32 devices in a mesh: prec: 16 (over z, x, core), run: 2 (over y).
Axes of the slice: x: 2, y: 2, z: 4, core: 2. Of those that a mesh axis runs over, the one named last changes fastest.
Arguments:
- intensity: bfloat16 [1024, 32768], P('run', 'prec'), may hold values from -6 to 6
- observed: int32 [1024, 4096], P('run', 'prec'), may hold values from 0 to 255, as said below
- run_factors: bfloat16 [1024, 64], P('run'), as said below
- prec_factors: bfloat16 [32768, 64], P('prec'), as said below
Outputs:
- completed: bfloat16 [1024, 32768], P('run', 'prec')
The draws below stay inside these ranges and needn't reach their ends.
Inputs may be any that keep to these rules, and one draw needn't show every extreme that they name: `observed`: each word packs eight observation flags in its low 8 bits: bit b of word j is the flag of precursor 8 j + b. `run_factors`: rows of the starting factors have scales that vary along the rows. `prec_factors`: rows of the starting factors have scales that vary along the rows.
All inputs are finite; a program needn't handle non-finite values.
Results may differ from the reference program's by a relative error of at most 0.005.
Values may be sent and summed in bfloat16 or wider, within the bound.
A program may use at most 64 MiB of HBM per device.

```python
import jax
import jax.numpy as jnp
from jax import lax

P_SIZE = 32768
K = 64
ITERS = 4
R = 1024


def scaled_rows(key, rows, cols):
    base = jax.random.normal(key, (rows, cols), jnp.float32)
    place = jnp.arange(rows, dtype=jnp.float32) / rows
    scale = 0.25 * jnp.exp(jnp.log(3.0) * place)
    return (base * scale[:, None]).astype(jnp.bfloat16)


def draw_run_factors(key, part):
    return scaled_rows(jax.random.fold_in(key, 11), R, K)


def draw_prec_factors(key, part):
    return scaled_rows(jax.random.fold_in(key, 23), P_SIZE, K)


def draw_observed(key, part):
    base = jax.random.fold_in(key, 37)
    words = P_SIZE // 8
    first = jax.random.randint(jax.random.fold_in(base, 1), (R, words), 0, 256)
    second = jax.random.randint(jax.random.fold_in(base, 2), (R, words), 0, 256)
    third = jax.random.randint(jax.random.fold_in(base, 3), (R, words), 0, 256)
    packed = first | second | third
    window = jax.random.randint(jax.random.fold_in(base, 4), (R // 64, words), 0, 5)
    keep = jnp.repeat((window != 0).astype(jnp.int32), 64, axis=0)
    result = (packed * keep).astype(jnp.int32)
    result = result.at[0, 0].set(255)
    result = result.at[R - 1, words - 1].set(0)
    return result


def block_levels(key, dims, shards, low, top_value):
    def one(position, blocks):
        heights = jax.random.uniform(jax.random.fold_in(jax.random.fold_in(key, 6), position), (blocks,), jnp.float32, low / len(shards), top_value / len(shards))
        return jnp.repeat(jnp.exp(heights), dims[position] // blocks).reshape((-1,) + (1,) * (len(dims) - position - 1))

    factor_of = one(*shards[0])
    for cut in shards[1:]:
        factor_of = factor_of * one(*cut)
    return factor_of


def gaussian(rng, extent, scale, reach, shards=(), kind=jnp.bfloat16):
    factor_of = block_levels(rng, extent, shards, -0.22, 0.18) if shards else 1.0
    drawn = jax.random.normal(rng, extent, jnp.float32) * scale * factor_of
    return jnp.minimum(jnp.maximum(drawn, -reach), reach).astype(kind)


def setup_inputs(seed: int = 0) -> dict:
    splits = jax.random.split(jax.random.key(seed), 5)
    intensity = gaussian(splits[0], (R, P_SIZE), 1.0, 6.0, ((0, 2), (1, 16)))
    observed = draw_observed(jax.random.fold_in(splits[4], 71), 0)
    run_factors = draw_run_factors(jax.random.fold_in(splits[4], 71), 0)
    prec_factors = draw_prec_factors(jax.random.fold_in(splits[4], 71), 0)
    return {"intensity": intensity, "observed": observed, "run_factors": run_factors, "prec_factors": prec_factors}


ridge_value = 16.0
block_rows = 1024

def unpack_mask(words):
    shifts = jnp.arange(8, dtype=jnp.int32)
    bits = jnp.right_shift(words[:, :, None], shifts) & 1
    return bits.reshape(words.shape[0], -1).astype(jnp.float32)

def ridge_solve(matrix, gram):
    size = gram.shape[0]
    factor = jnp.linalg.cholesky(gram + ridge_value * jnp.eye(size, dtype=jnp.float32))
    return jax.scipy.linalg.cho_solve((factor, True), matrix.T).T

def reference(intensity, observed, run_factors, prec_factors):
    rows_all = intensity.shape[0]
    block = min(block_rows, rows_all)
    nblocks = rows_all // block
    inten_blocks = intensity.reshape(nblocks, block, -1)
    mask_blocks = observed.reshape(nblocks, block, -1)
    u_now = run_factors
    v_now = prec_factors
    for step in range(ITERS):
        gram_v = jnp.dot(v_now.T.astype(jnp.float32), v_now.astype(jnp.float32), preferred_element_type=jnp.float32)
        u_blocks = u_now.reshape(nblocks, block, -1)

        def update_u(items):
            inten, words, u_blk = items
            fit = jnp.dot(u_blk.astype(jnp.float32), v_now.T.astype(jnp.float32), preferred_element_type=jnp.float32)
            resid = (unpack_mask(words) * (inten.astype(jnp.float32) - fit)).astype(jnp.bfloat16)
            proj = jnp.dot(resid.astype(jnp.float32), v_now.astype(jnp.float32), preferred_element_type=jnp.float32)
            total = jnp.dot(u_blk.astype(jnp.float32), gram_v, precision=lax.Precision.HIGHEST) + proj
            return ridge_solve(total, gram_v).astype(jnp.bfloat16)
        u_now = lax.map(update_u, (inten_blocks, mask_blocks, u_blocks)).reshape(rows_all, -1)
        gram_u = jnp.dot(u_now.T.astype(jnp.float32), u_now.astype(jnp.float32), preferred_element_type=jnp.float32)
        u_blocks = u_now.reshape(nblocks, block, -1)

        def add_proj(carry, items):
            inten, words, u_blk = items
            fit = jnp.dot(u_blk.astype(jnp.float32), v_now.T.astype(jnp.float32), preferred_element_type=jnp.float32)
            resid = (unpack_mask(words) * (inten.astype(jnp.float32) - fit)).astype(jnp.bfloat16)
            return (carry + jnp.dot(resid.T.astype(jnp.float32), u_blk.astype(jnp.float32), preferred_element_type=jnp.float32), None)
        start = jnp.zeros(v_now.shape, jnp.float32)
        proj_v, unused = lax.scan(add_proj, start, (inten_blocks, mask_blocks, u_blocks))
        total = jnp.dot(v_now.astype(jnp.float32), gram_u, precision=lax.Precision.HIGHEST) + proj_v
        v_now = ridge_solve(total, gram_u).astype(jnp.bfloat16)
    u_blocks = u_now.reshape(nblocks, block, -1)

    def finish(items):
        inten, words, u_blk = items
        fit = jnp.dot(u_blk.astype(jnp.float32), v_now.T.astype(jnp.float32), preferred_element_type=jnp.float32)
        maskf = unpack_mask(words)
        return (maskf * inten.astype(jnp.float32) + (1.0 - maskf) * fit).astype(jnp.bfloat16)
    return lax.map(finish, (inten_blocks, mask_blocks, u_blocks)).reshape(rows_all, -1)
```

```python
import functools

import jax
import jax.numpy as jnp
from jax import lax
from jax.experimental import pallas as pl
from jax.experimental.pallas import tpu as pltpu
from jax.sharding import PartitionSpec as P

ITERS = 4
ridge_value = 16.0
f32 = jnp.float32
bf16 = jnp.bfloat16
MESH = pl.DeviceIdType.MESH
VMEM_LIMIT = 67043328
MISSING = 2.0**100
PRESENT = 2.0**90


def mm(a, b):
    return lax.dot_general(a, b, (((1,), (0,)), ((), ())), preferred_element_type=f32)


def mm_nt(a, b):
    return lax.dot_general(a, b, (((1,), (1,)), ((), ())), preferred_element_type=f32)


def spd_inverse(a):
    size = a.shape[0]
    wide = 2 * size
    rid = lax.broadcasted_iota(jnp.int32, (size, wide), 0)
    eye = (
        lax.broadcasted_iota(jnp.int32, (size, size), 0)
        == lax.broadcasted_iota(jnp.int32, (size, size), 1)
    ).astype(f32)
    m = jnp.concatenate([a + ridge_value * eye, eye], axis=1)
    group = 4
    for k0 in range(0, size, group):
        cols = [
            jnp.broadcast_to(m[:, k0 + j : k0 + j + 1], (size, wide)) for j in range(group)
        ]
        for j in range(group):
            k = k0 + j
            inv = 1.0 / cols[j][k : k + 1, :]
            prow = m[k : k + 1, :] * inv
            m = jnp.where(rid == k, prow, m - cols[j] * prow)
            for n in range(j + 1, group):
                f = cols[j][k0 + n : k0 + n + 1, :] * inv
                cols[n] = jnp.where(rid == k, f, cols[n] - cols[j] * f)
    return m[:, size:]


def split(x):
    hi = x.astype(bf16)
    return hi, (x - hi.astype(f32)).astype(bf16)


def pack_gram(g):
    h = g.shape[0] // 2
    return jnp.concatenate([g[:h], g[h:]], axis=1)


def unpack_gram(x):
    h = x.shape[1] // 2
    return jnp.concatenate([x[:, :h], x[:, h:]], axis=0)


def als_kernel(
    n, nr, owners, vchunks,
    x_hbm, w_hbm, ut0_hbm, vt0_hbm, out_ref,
    x_ref, w_ref, ut0_ref, u, ub, vt, pacc, gsend, grecv, gtot, psend, precv, tb, gu, pv,
    xs, wsem, vs, g1s, g1r, g2s, g2r, ps, pr, ts, tr, gus, gur, pvs, pvr,
):
    me = lax.axis_index("prec")
    my = lax.axis_index("run")
    k, cols = vt.shape
    rows = u.shape[0]
    half = rows // 2
    sp = half // owners
    gowners = gsend.shape[0]
    cw = cols // vchunks
    base, stride = n // 4, n // 2 // owners
    others = [lax.rem(me + off, n) for off in range(1, n)]
    rothers = [lax.rem(my + off, nr) for off in range(1, nr)]
    offset = me - base
    seat = lax.div(offset, stride)
    owns = (offset >= 0) & (offset < owners * stride) & (offset == seat * stride)
    gowns = owns & (seat < gowners)

    nb = xs.shape[0]
    rb = rows // nb
    vload = pltpu.make_async_copy(vt0_hbm, vt, vs.at[0])
    uload = pltpu.make_async_copy(ut0_hbm, ut0_ref, vs.at[1])
    xload, wload = [], []
    for i in range(nb):
        span = slice(i * rb, (i + 1) * rb)
        wload.append(pltpu.make_async_copy(w_hbm.at[span], w_ref.at[span], wsem.at[i]))
        xload.append(pltpu.make_async_copy(x_hbm.at[span], x_ref.at[span], xs.at[i]))
    vload.start()
    uload.start()
    for i in range(nb):
        wload[i].start()
        xload[i].start()
    barrier = pltpu.get_barrier_semaphore()
    for d in others:
        pl.semaphore_signal(barrier, inc=1, device_id={"prec": d}, device_id_type=MESH)
    for d in rothers:
        pl.semaphore_signal(barrier, inc=1, device_id={"run": d}, device_id_type=MESH)

    def rcopy(src, dst, ss, rs, axis, d):
        return pltpu.make_async_remote_copy(
            src_ref=src, dst_ref=dst, send_sem=ss, recv_sem=rs,
            device_id={axis: d}, device_id_type=MESH,
        )

    def place(o):
        return base + o * stride

    eye = (
        lax.broadcasted_iota(jnp.int32, (k, k), 0) == lax.broadcasted_iota(jnp.int32, (k, k), 1)
    ).astype(f32).astype(bf16)

    vload.wait()
    uload.wait()
    start = jnp.transpose(ut0_ref[...].astype(f32))
    u[...] = start.astype(bf16)
    ub[...] = (
        jnp.concatenate([start[:half], start[half:]], axis=1).astype(bf16).reshape(ub.shape)
    )

    words = w_ref.shape[1]
    wb = min(128, words)
    spread = (
        lax.broadcasted_iota(jnp.int32, (wb, 8 * wb), 0)
        == lax.broadcasted_iota(jnp.int32, (wb, 8 * wb), 1) // 8
    ).astype(f32).astype(bf16)
    bit = jnp.left_shift(1, lax.broadcasted_iota(jnp.int32, (rb, 8 * wb), 1) & 7)
    for i in range(nb):
        r0, r1 = i * rb, (i + 1) * rb
        wload[i].wait()
        xload[i].wait()
        for c in range(words // wb):
            part = w_ref[r0:r1, c * wb : (c + 1) * wb].astype(f32).astype(bf16)
            seen = (mm(part, spread).astype(jnp.int32) & bit) != 0
            x = x_ref[r0:r1, c * 8 * wb : (c + 1) * 8 * wb].astype(f32)
            x_ref[r0:r1, c * 8 * wb : (c + 1) * 8 * wb] = jnp.where(seen, x, MISSING).astype(bf16)

    present = jnp.asarray(PRESENT, bf16)

    def resid(c0, c1, fit):
        x = x_ref[:, c0:c1]
        return jnp.where(x < present, (x.astype(f32) - fit).astype(bf16), jnp.zeros_like(x))

    def g1(o, d):
        return rcopy(gsend.at[o], grecv.at[d], g1s.at[o], g1r.at[d], "prec", place(o))

    def g2(o, d):
        return rcopy(gtot.at[o], gtot.at[o], g2s.at[d], g2r.at[o], "prec", d)

    def p1(o, d):
        return rcopy(psend.at[o], precv.at[d], ps.at[o], pr.at[d], "prec", place(o))

    def t1(o, d):
        return rcopy(tb.at[o], tb.at[o], ts.at[d], tr.at[o], "prec", d)

    def each_owner(count, act):
        for j in range(count):
            o = lax.rem(me + j, count)

            @pl.when(place(o) != me)
            def _():
                act(o)

    def launch_u(update):
        gram = None
        for c in range(vchunks):
            c0, c1 = c * cw, (c + 1) * cw
            if update is not None:
                update(c)
            v = vt[:, c0:c1]
            gram = mm_nt(v, v) if gram is None else gram + mm_nt(v, v)
            if c == vchunks - 1:
                gsend[...] = pack_gram(gram).reshape(gsend.shape)
                each_owner(gowners, lambda o: g1(o, me).start())
            proj = mm_nt(resid(c0, c1, mm(u[...], v)), v)
            pacc[...] = proj if c == 0 else pacc[...] + proj
        both = jnp.concatenate([pacc[:half], pacc[half:]], axis=1)
        psend[...] = both.astype(bf16).reshape(psend.shape)
        each_owner(owners, lambda o: p1(o, me).start())

    def finish_u():
        @pl.when(gowns)
        def _():
            for d in others:
                g1(seat, d).wait_recv()
            grecv[me] = gsend[seat]
            total = grecv[0]
            for d in range(1, n):
                total = total + grecv[d]
            gtot[seat] = total
            for d in others:
                g2(seat, d).start()

        @pl.when(owns)
        def _():
            for d in others:
                p1(seat, d).wait_recv()
            total = psend[seat].astype(f32)
            for d in others:
                total = total + precv[d].astype(f32)
            tb[seat] = (total - ridge_value * ub[seat].astype(f32)).astype(bf16)
            for d in others:
                t1(seat, d).start()

        each_owner(gowners, lambda o: g2(o, me).wait_recv())
        ihi, ilo = split(spd_inverse(unpack_gram(gtot[...].reshape(k // 2, 2 * k))))
        none = jnp.zeros_like(ihi)
        rhs = jnp.concatenate(
            [jnp.concatenate(r, axis=1) for r in ((ihi, none), (none, ihi), (ilo, none), (none, ilo))],
            axis=0,
        )
        each_owner(owners, lambda o: t1(o, me).wait_recv())
        t = tb[...].reshape(half, 2 * k)
        step = mm(jnp.concatenate([t, t], axis=1), rhs)
        new = (ub[...].reshape(half, 2 * k).astype(f32) + step).astype(bf16)
        ub[...] = new.reshape(ub.shape)
        u[:half] = new[:, :k]
        u[half:] = new[:, k:]
        each_owner(gowners, lambda o: g1(o, me).wait_send())
        each_owner(owners, lambda o: p1(o, me).wait_send())

        @pl.when(gowns)
        def _():
            for d in others:
                g2(seat, d).wait_send()

        @pl.when(owns)
        def _():
            for d in others:
                t1(seat, d).wait_send()

    def launch_v(par):
        now = u[...]
        ut = mm_nt(eye, now).astype(bf16)
        for c in range(vchunks):
            c0, c1 = c * cw, (c + 1) * cw
            fit = mm(now, vt[:, c0:c1])
            pv[par, my, c] = mm(ut, resid(c0, c1, fit)).astype(bf16)
            for d in rothers:
                mine = pv.at[par, my, c]
                rcopy(mine, mine, pvs.at[d, c], pvr.at[par, my, c], "run", d).start()
            if c == 0:
                gu[par, my] = pack_gram(mm_nt(ut, ut))
                for d in rothers:
                    rcopy(gu.at[par, my], gu.at[par, my], gus.at[d], gur.at[par, my], "run", d).start()
        for d in rothers:
            rcopy(gu.at[par, my], gu.at[par, d], gus.at[d], gur.at[par, d], "run", d).wait()
        total = gu[par, 0]
        for d in range(1, nr):
            total = total + gu[par, d]
        ihi, ilo = split(spd_inverse(unpack_gram(total)))
        lhs = jnp.concatenate([ihi, ilo, ihi], axis=1)

        def update(c):
            c0, c1 = c * cw, (c + 1) * cw
            for d in rothers:
                rcopy(
                    pv.at[par, my, c], pv.at[par, d, c], pvs.at[d, c], pvr.at[par, d, c], "run", d
                ).wait()
            share = pv[par, 0, c].astype(f32)
            for d in range(1, nr):
                share = share + pv[par, d, c].astype(f32)
            old = vt[:, c0:c1].astype(f32)
            dhi, dlo = split(share - ridge_value * old)
            step = mm(lhs, jnp.concatenate([dhi, dhi, dlo], axis=0))
            vt[:, c0:c1] = (old + step).astype(bf16)

        return update

    pl.semaphore_wait(barrier, n - 1 + nr - 1)
    launch_u(None)

    def iteration(it, carry):
        finish_u()
        launch_u(launch_v(lax.rem(it, 2)))
        return carry

    lax.fori_loop(0, ITERS - 1, iteration, 0)
    finish_u()
    update = launch_v((ITERS - 1) % 2)
    for c in range(vchunks):
        c0, c1 = c * cw, (c + 1) * cw
        update(c)
        fit = mm(u[...], vt[:, c0:c1]).astype(bf16)
        x = x_ref[:, c0:c1]
        out_ref[:, c0:c1] = jnp.where(x < present, x, fit)


def local(n, nr, intensity, observed, run_factors, prec_factors):
    rows, cols = intensity.shape
    words = observed.shape[1]
    k = run_factors.shape[1]
    half = rows // 2
    owners = max(1, min(n // 2, half // 32))
    sp = half // owners
    gowners = max(1, min(owners, k // 16))
    gr = k // 2 // gowners
    vchunks = max(1, min(4, cols // 128))
    cw = cols // vchunks
    nb = max(1, rows // 128)
    dma = pltpu.SemaphoreType.DMA
    hbm = pl.BlockSpec(memory_space=pltpu.HBM)
    return pl.pallas_call(
        functools.partial(als_kernel, n, nr, owners, vchunks),
        out_shape=jax.ShapeDtypeStruct((rows, cols), bf16),
        in_specs=[hbm] * 4,
        out_specs=pl.BlockSpec(memory_space=pltpu.VMEM),
        scratch_shapes=[
            pltpu.VMEM((rows, cols), bf16),
            pltpu.VMEM((rows, words), jnp.int32),
            pltpu.VMEM((k, rows), bf16),
            pltpu.VMEM((rows, k), bf16),
            pltpu.VMEM((owners, sp, 2 * k), bf16),
            pltpu.VMEM((k, cols), bf16),
            pltpu.VMEM((rows, k), f32),
            pltpu.VMEM((gowners, gr, 2 * k), f32),
            pltpu.VMEM((n, gr, 2 * k), f32),
            pltpu.VMEM((gowners, gr, 2 * k), f32),
            pltpu.VMEM((owners, sp, 2 * k), bf16),
            pltpu.VMEM((n, sp, 2 * k), bf16),
            pltpu.VMEM((owners, sp, 2 * k), bf16),
            pltpu.VMEM((2, nr, k // 2, 2 * k), f32),
            pltpu.VMEM((2, nr, vchunks, k, cw), bf16),
            dma((nb,)), dma((nb,)), dma((2,)),
            dma((gowners,)), dma((n,)), dma((n,)), dma((gowners,)),
            dma((owners,)), dma((n,)), dma((n,)), dma((owners,)),
            dma((nr,)), dma((2, nr)), dma((nr, vchunks)), dma((2, nr, vchunks)),
        ],
        compiler_params=pltpu.CompilerParams(
            collective_id=0, has_side_effects=True, vmem_limit_bytes=VMEM_LIMIT
        ),
    )(intensity, observed, run_factors.T, prec_factors.T)


def solution(mesh):
    n, nr = mesh.shape["prec"], mesh.shape["run"]
    return jax.shard_map(
        functools.partial(local, n, nr),
        mesh=mesh,
        in_specs=(P("run", "prec"), P("run", "prec"), P("run", None), P("prec", None)),
        out_specs=P("run", "prec"),
        check_vma=False,
    )
```

```python
import functools

import jax
import jax.numpy as jnp
from jax import lax
from jax.experimental import pallas as pl
from jax.experimental.pallas import tpu as pltpu
from jax.sharding import PartitionSpec as P

ITERS = 4
ridge_value = 16.0
f32 = jnp.float32
bf16 = jnp.bfloat16
MESH = pl.DeviceIdType.MESH
VMEM_LIMIT = 32 << 20
MISSING = 2.0**100
PRESENT = 2.0**90


def mm(a, b):
    return lax.dot_general(a, b, (((1,), (0,)), ((), ())), preferred_element_type=f32)


def mm_nt(a, b):
    return lax.dot_general(a, b, (((1,), (1,)), ((), ())), preferred_element_type=f32)


def spd_inverse(a):
    size = a.shape[0]
    wide = 2 * size
    rid = lax.broadcasted_iota(jnp.int32, (size, wide), 0)
    eye = (
        lax.broadcasted_iota(jnp.int32, (size, size), 0)
        == lax.broadcasted_iota(jnp.int32, (size, size), 1)
    ).astype(f32)
    m = jnp.concatenate([a + ridge_value * eye, eye], axis=1)
    group = 4
    for k0 in range(0, size, group):
        cols = [
            jnp.broadcast_to(m[:, k0 + j : k0 + j + 1], (size, wide)) for j in range(group)
        ]
        for j in range(group):
            k = k0 + j
            inv = 1.0 / cols[j][k : k + 1, :]
            prow = m[k : k + 1, :] * inv
            m = jnp.where(rid == k, prow, m - cols[j] * prow)
            for n in range(j + 1, group):
                f = cols[j][k0 + n : k0 + n + 1, :] * inv
                cols[n] = jnp.where(rid == k, f, cols[n] - cols[j] * f)
    return m[:, size:]


def split(x):
    hi = x.astype(bf16)
    return hi, (x - hi.astype(f32)).astype(bf16)


def pack_gram(g):
    h = g.shape[0] // 2
    return jnp.concatenate([g[:h], g[h:]], axis=1)


def unpack_gram(x):
    h = x.shape[1] // 2
    return jnp.concatenate([x[:, :h], x[:, h:]], axis=0)


def als_kernel(
    n, nr, owners, vchunks,
    x_hbm, w_hbm, ut0_hbm, vt0_hbm, out_ref,
    x_ref, w_ref, ut0_ref, u, ub, vt, pacc, gsend, grecv, gtot, psend, precv, tb, gu, pv,
    xs, wsem, vs, g1s, g1r, g2s, g2r, ps, pr, ts, tr, gus, gur, pvs, pvr,
):
    me = lax.axis_index("prec")
    my = lax.axis_index("run")
    k, cols = vt.shape
    rows = u.shape[0]
    half = rows // 2
    sp = half // owners
    gowners = gsend.shape[0]
    cw = cols // vchunks
    base, stride = n // 4, n // 2 // owners
    others = [lax.rem(me + off, n) for off in range(1, n)]
    rothers = [lax.rem(my + off, nr) for off in range(1, nr)]
    offset = me - base
    seat = lax.div(offset, stride)
    owns = (offset >= 0) & (offset < owners * stride) & (offset == seat * stride)
    gowns = owns & (seat < gowners)

    nb = xs.shape[0]
    rb = rows // nb
    vload = pltpu.make_async_copy(vt0_hbm, vt, vs.at[0])
    uload = pltpu.make_async_copy(ut0_hbm, ut0_ref, vs.at[1])
    xload, wload = [], []
    for i in range(nb):
        span = slice(i * rb, (i + 1) * rb)
        wload.append(pltpu.make_async_copy(w_hbm.at[span], w_ref.at[span], wsem.at[i]))
        xload.append(pltpu.make_async_copy(x_hbm.at[span], x_ref.at[span], xs.at[i]))
    vload.start()
    uload.start()
    for i in range(nb):
        wload[i].start()
        xload[i].start()
    barrier = pltpu.get_barrier_semaphore()
    for d in others:
        pl.semaphore_signal(barrier, inc=1, device_id={"prec": d}, device_id_type=MESH)
    for d in rothers:
        pl.semaphore_signal(barrier, inc=1, device_id={"run": d}, device_id_type=MESH)

    def rcopy(src, dst, ss, rs, axis, d):
        return pltpu.make_async_remote_copy(
            src_ref=src, dst_ref=dst, send_sem=ss, recv_sem=rs,
            device_id={axis: d}, device_id_type=MESH,
        )

    def place(o):
        return base + o * stride

    eye = (
        lax.broadcasted_iota(jnp.int32, (k, k), 0) == lax.broadcasted_iota(jnp.int32, (k, k), 1)
    ).astype(f32).astype(bf16)

    vload.wait()
    uload.wait()
    start = jnp.transpose(ut0_ref[...].astype(f32))
    u[...] = start.astype(bf16)
    ub[...] = (
        jnp.concatenate([start[:half], start[half:]], axis=1).astype(bf16).reshape(ub.shape)
    )

    words = w_ref.shape[1]
    wb = min(128, words)
    spread = (
        lax.broadcasted_iota(jnp.int32, (wb, 8 * wb), 0)
        == lax.broadcasted_iota(jnp.int32, (wb, 8 * wb), 1) // 8
    ).astype(f32).astype(bf16)
    bit = jnp.left_shift(1, lax.broadcasted_iota(jnp.int32, (rb, 8 * wb), 1) & 7)
    for i in range(nb):
        r0, r1 = i * rb, (i + 1) * rb
        wload[i].wait()
        xload[i].wait()
        for c in range(words // wb):
            part = w_ref[r0:r1, c * wb : (c + 1) * wb].astype(f32).astype(bf16)
            seen = (mm(part, spread).astype(jnp.int32) & bit) != 0
            x = x_ref[r0:r1, c * 8 * wb : (c + 1) * 8 * wb].astype(f32)
            x_ref[r0:r1, c * 8 * wb : (c + 1) * 8 * wb] = jnp.where(seen, x, MISSING).astype(bf16)

    present = jnp.asarray(PRESENT, bf16)

    def resid(c0, c1, fit):
        x = x_ref[:, c0:c1]
        return jnp.where(x < present, (x.astype(f32) - fit).astype(bf16), jnp.zeros_like(x))

    def g1(o, d):
        return rcopy(gsend.at[o], grecv.at[d], g1s.at[o], g1r.at[d], "prec", place(o))

    def g2(o, d):
        return rcopy(gtot.at[o], gtot.at[o], g2s.at[d], g2r.at[o], "prec", d)

    def p1(o, d):
        return rcopy(psend.at[o], precv.at[d], ps.at[o], pr.at[d], "prec", place(o))

    def t1(o, d):
        return rcopy(tb.at[o], tb.at[o], ts.at[d], tr.at[o], "prec", d)

    def each_owner(count, act):
        for j in range(count):
            o = lax.rem(me + j, count)

            @pl.when(place(o) != me)
            def _():
                act(o)

    def launch_u(update):
        gram = None
        for c in range(vchunks):
            c0, c1 = c * cw, (c + 1) * cw
            if update is not None:
                update(c)
            v = vt[:, c0:c1]
            gram = mm_nt(v, v) if gram is None else gram + mm_nt(v, v)
            if c == vchunks - 1:
                gsend[...] = pack_gram(gram).reshape(gsend.shape)
                each_owner(gowners, lambda o: g1(o, me).start())
            proj = mm_nt(resid(c0, c1, mm(u[...], v)), v)
            pacc[...] = proj if c == 0 else pacc[...] + proj
        both = jnp.concatenate([pacc[:half], pacc[half:]], axis=1)
        psend[...] = both.astype(bf16).reshape(psend.shape)
        each_owner(owners, lambda o: p1(o, me).start())

    def finish_u():
        @pl.when(gowns)
        def _():
            for d in others:
                g1(seat, d).wait_recv()
            grecv[me] = gsend[seat]
            total = grecv[0]
            for d in range(1, n):
                total = total + grecv[d]
            gtot[seat] = total
            for d in others:
                g2(seat, d).start()

        @pl.when(owns)
        def _():
            for d in others:
                p1(seat, d).wait_recv()
            total = psend[seat].astype(f32)
            for d in others:
                total = total + precv[d].astype(f32)
            tb[seat] = (total - ridge_value * ub[seat].astype(f32)).astype(bf16)
            for d in others:
                t1(seat, d).start()

        each_owner(gowners, lambda o: g2(o, me).wait_recv())
        ihi, ilo = split(spd_inverse(unpack_gram(gtot[...].reshape(k // 2, 2 * k))))
        none = jnp.zeros_like(ihi)
        rhs = jnp.concatenate(
            [jnp.concatenate(r, axis=1) for r in ((ihi, none), (none, ihi), (ilo, none), (none, ilo))],
            axis=0,
        )
        each_owner(owners, lambda o: t1(o, me).wait_recv())
        t = tb[...].reshape(half, 2 * k)
        step = mm(jnp.concatenate([t, t], axis=1), rhs)
        new = (ub[...].reshape(half, 2 * k).astype(f32) + step).astype(bf16)
        ub[...] = new.reshape(ub.shape)
        u[:half] = new[:, :k]
        u[half:] = new[:, k:]
        each_owner(gowners, lambda o: g1(o, me).wait_send())
        each_owner(owners, lambda o: p1(o, me).wait_send())

        @pl.when(gowns)
        def _():
            for d in others:
                g2(seat, d).wait_send()

        @pl.when(owns)
        def _():
            for d in others:
                t1(seat, d).wait_send()

    def launch_v(par):
        now = u[...]
        ut = mm_nt(eye, now).astype(bf16)
        for c in range(vchunks):
            c0, c1 = c * cw, (c + 1) * cw
            fit = mm(now, vt[:, c0:c1])
            pv[par, my, c] = mm(ut, resid(c0, c1, fit)).astype(bf16)
            for d in rothers:
                mine = pv.at[par, my, c]
                rcopy(mine, mine, pvs.at[d, c], pvr.at[par, my, c], "run", d).start()
            if c == 0:
                gu[par, my] = pack_gram(mm_nt(ut, ut))
                for d in rothers:
                    rcopy(gu.at[par, my], gu.at[par, my], gus.at[d], gur.at[par, my], "run", d).start()
        for d in rothers:
            rcopy(gu.at[par, my], gu.at[par, d], gus.at[d], gur.at[par, d], "run", d).wait()
        total = gu[par, 0]
        for d in range(1, nr):
            total = total + gu[par, d]
        ihi, ilo = split(spd_inverse(unpack_gram(total)))
        lhs = jnp.concatenate([ihi, ilo, ihi], axis=1)

        def update(c):
            c0, c1 = c * cw, (c + 1) * cw
            for d in rothers:
                rcopy(
                    pv.at[par, my, c], pv.at[par, d, c], pvs.at[d, c], pvr.at[par, d, c], "run", d
                ).wait()
            share = pv[par, 0, c].astype(f32)
            for d in range(1, nr):
                share = share + pv[par, d, c].astype(f32)
            old = vt[:, c0:c1].astype(f32)
            dhi, dlo = split(share - ridge_value * old)
            step = mm(lhs, jnp.concatenate([dhi, dhi, dlo], axis=0))
            vt[:, c0:c1] = (old + step).astype(bf16)

        return update

    pl.semaphore_wait(barrier, n - 1 + nr - 1)
    launch_u(None)

    def iteration(it, carry):
        finish_u()
        launch_u(launch_v(lax.rem(it, 2)))
        return carry

    lax.fori_loop(0, ITERS - 1, iteration, 0)
    finish_u()
    update = launch_v((ITERS - 1) % 2)
    for c in range(vchunks):
        c0, c1 = c * cw, (c + 1) * cw
        update(c)
        fit = mm(u[...], vt[:, c0:c1]).astype(bf16)
        x = x_ref[:, c0:c1]
        out_ref[:, c0:c1] = jnp.where(x < present, x, fit)


def local(n, nr, intensity, observed, run_factors, prec_factors):
    rows, cols = intensity.shape
    words = observed.shape[1]
    k = run_factors.shape[1]
    half = rows // 2
    owners = max(1, min(n // 2, half // 32))
    sp = half // owners
    gowners = max(1, min(owners, k // 16))
    gr = k // 2 // gowners
    vchunks = max(1, min(4, cols // 128))
    cw = cols // vchunks
    nb = max(1, rows // 128)
    dma = pltpu.SemaphoreType.DMA
    hbm = pl.BlockSpec(memory_space=pltpu.HBM)
    operands = (intensity, observed, run_factors.T, prec_factors.T)
    return pl.pallas_call(
        functools.partial(als_kernel, n, nr, owners, vchunks),
        out_shape=jax.ShapeDtypeStruct((rows, cols), bf16),
        in_specs=[hbm] * 4,
        out_specs=pl.BlockSpec(memory_space=pltpu.VMEM),
        scratch_shapes=[
            pltpu.VMEM((rows, cols), bf16),
            pltpu.VMEM((rows, words), jnp.int32),
            pltpu.VMEM((k, rows), bf16),
            pltpu.VMEM((rows, k), bf16),
            pltpu.VMEM((owners, sp, 2 * k), bf16),
            pltpu.VMEM((k, cols), bf16),
            pltpu.VMEM((rows, k), f32),
            pltpu.VMEM((gowners, gr, 2 * k), f32),
            pltpu.VMEM((n, gr, 2 * k), f32),
            pltpu.VMEM((gowners, gr, 2 * k), f32),
            pltpu.VMEM((owners, sp, 2 * k), bf16),
            pltpu.VMEM((n, sp, 2 * k), bf16),
            pltpu.VMEM((owners, sp, 2 * k), bf16),
            pltpu.VMEM((2, nr, k // 2, 2 * k), f32),
            pltpu.VMEM((2, nr, vchunks, k, cw), bf16),
            dma((nb,)), dma((nb,)), dma((2,)),
            dma((gowners,)), dma((n,)), dma((n,)), dma((gowners,)),
            dma((owners,)), dma((n,)), dma((n,)), dma((owners,)),
            dma((nr,)), dma((2, nr)), dma((nr, vchunks)), dma((2, nr, vchunks)),
        ],
        compiler_params=pltpu.CompilerParams(
            collective_id=0, has_side_effects=True, vmem_limit_bytes=VMEM_LIMIT
        ),
    )(*(pltpu.with_memory_space_constraint(a, pltpu.HBM) for a in operands))


def solution(mesh):
    n, nr = mesh.shape["prec"], mesh.shape["run"]
    return jax.shard_map(
        functools.partial(local, n, nr),
        mesh=mesh,
        in_specs=(P("run", "prec"), P("run", "prec"), P("run", None), P("prec", None)),
        out_specs=P("run", "prec"),
        check_vma=False,
    )
```

```python
import functools

import jax
import jax.numpy as jnp
from jax import lax
from jax.experimental import pallas as pl
from jax.experimental.pallas import tpu as pltpu
from jax.sharding import PartitionSpec as P

ITERS = 4
ridge_value = 16.0
f32 = jnp.float32
bf16 = jnp.bfloat16
MESH = pl.DeviceIdType.MESH
VMEM_LIMIT = 32 << 20
MISSING = 2.0**100
PRESENT = 2.0**90


def mm(a, b):
    return lax.dot_general(a, b, (((1,), (0,)), ((), ())), preferred_element_type=f32)


def mm_nt(a, b):
    return lax.dot_general(a, b, (((1,), (1,)), ((), ())), preferred_element_type=f32)


def tree_sum(terms):
    while len(terms) > 1:
        terms = [sum(terms[i : i + 2]) for i in range(0, len(terms), 2)]
    return terms[0]


def spd_inverse(a):
    size = a.shape[0]
    wide = 2 * size
    eye = (
        lax.broadcasted_iota(jnp.int32, (size, size), 0)
        == lax.broadcasted_iota(jnp.int32, (size, size), 1)
    ).astype(f32)
    full = jnp.concatenate([a + ridge_value * eye, eye], axis=1)
    m = [full[i : i + 8] for i in range(0, size, 8)]
    row = lax.broadcasted_iota(jnp.int32, (8, wide), 0)

    def col(block, j):
        return jnp.broadcast_to(block[:, j : j + 1], (8, wide))

    for q in range(size // 8):
        pivot = m[q]
        cols = [col(pivot, 8 * q + j) for j in range(8)]
        for j in range(0, 8, 2):
            c0, c1 = cols[j], cols[j + 1]
            p00, p10, p01, p11 = c0[j : j + 1], c0[j + 1 : j + 2], c1[j : j + 1], c1[j + 1 : j + 2]
            inv = 1.0 / (p00 * p11 - p01 * p10)
            i00, i01, i10, i11 = p11 * inv, p01 * inv, p10 * inv, p00 * inv

            def eliminate(v):
                r0, r1 = v[j : j + 1], v[j + 1 : j + 2]
                x0, x1 = i00 * r0 - i01 * r1, i11 * r1 - i10 * r0
                rest = v - (c0 * x0 + c1 * x1)
                return jnp.where(row == j, x0, jnp.where(row == j + 1, x1, rest))

            cols = cols[: j + 2] + [eliminate(v) for v in cols[j + 2 :]]
            pivot = eliminate(pivot)
        m = [
            pivot
            if i == q
            else m[i] - tree_sum([col(m[i], 8 * q + j) * pivot[j : j + 1] for j in range(8)])
            for i in range(size // 8)
        ]
    return jnp.concatenate(m, axis=0)[:, size:]


def split(x):
    hi = x.astype(bf16)
    return hi, (x - hi.astype(f32)).astype(bf16)


def pack_gram(g):
    h = g.shape[0] // 2
    return jnp.concatenate([g[:h], g[h:]], axis=1)


def unpack_gram(x):
    h = x.shape[1] // 2
    return jnp.concatenate([x[:, :h], x[:, h:]], axis=0)


def als_kernel(
    n, nr, owners, vchunks,
    x_hbm, w_hbm, ut0_hbm, vt0_hbm, out_ref,
    x_ref, w_ref, ut0_ref, u, ub, vt, pacc, gsend, grecv, gtot, psend, precv, tb, gu, pv,
    xs, wsem, vs, g1s, g1r, g2s, g2r, ps, pr, ts, tr, gus, gur, pvs, pvr,
):
    me = lax.axis_index("prec")
    my = lax.axis_index("run")
    k, cols = vt.shape
    rows = u.shape[0]
    half = rows // 2
    sp = half // owners
    gowners = gsend.shape[0]
    cw = cols // vchunks
    base, stride = n // 4, n // 2 // owners
    others = [lax.rem(me + off, n) for off in range(1, n)]
    rothers = [lax.rem(my + off, nr) for off in range(1, nr)]
    offset = me - base
    seat = lax.div(offset, stride)
    owns = (offset >= 0) & (offset < owners * stride) & (offset == seat * stride)
    gowns = owns & (seat < gowners)

    nb = xs.shape[0]
    rb = rows // nb
    vload = pltpu.make_async_copy(vt0_hbm, vt, vs.at[0])
    uload = pltpu.make_async_copy(ut0_hbm, ut0_ref, vs.at[1])
    xload, wload = [], []
    for i in range(nb):
        span = slice(i * rb, (i + 1) * rb)
        wload.append(pltpu.make_async_copy(w_hbm.at[span], w_ref.at[span], wsem.at[i]))
        xload.append(pltpu.make_async_copy(x_hbm.at[span], x_ref.at[span], xs.at[i]))
    vload.start()
    uload.start()
    for i in range(nb):
        wload[i].start()
        xload[i].start()
    barrier = pltpu.get_barrier_semaphore()
    for d in others:
        pl.semaphore_signal(barrier, inc=1, device_id={"prec": d}, device_id_type=MESH)
    for d in rothers:
        pl.semaphore_signal(barrier, inc=1, device_id={"run": d}, device_id_type=MESH)

    def rcopy(src, dst, ss, rs, axis, d):
        return pltpu.make_async_remote_copy(
            src_ref=src, dst_ref=dst, send_sem=ss, recv_sem=rs,
            device_id={axis: d}, device_id_type=MESH,
        )

    def place(o):
        return base + o * stride

    eye = (
        lax.broadcasted_iota(jnp.int32, (k, k), 0) == lax.broadcasted_iota(jnp.int32, (k, k), 1)
    ).astype(f32).astype(bf16)

    vload.wait()
    uload.wait()
    start = jnp.transpose(ut0_ref[...].astype(f32))
    u[...] = start.astype(bf16)
    ub[...] = (
        jnp.concatenate([start[:half], start[half:]], axis=1).astype(bf16).reshape(ub.shape)
    )

    words = w_ref.shape[1]
    wb = min(128, words)
    spread = (
        lax.broadcasted_iota(jnp.int32, (wb, 8 * wb), 0)
        == lax.broadcasted_iota(jnp.int32, (wb, 8 * wb), 1) // 8
    ).astype(f32).astype(bf16)
    bit = jnp.left_shift(1, lax.broadcasted_iota(jnp.int32, (rb, 8 * wb), 1) & 7)
    for i in range(nb):
        r0, r1 = i * rb, (i + 1) * rb
        wload[i].wait()
        xload[i].wait()
        for c in range(words // wb):
            part = w_ref[r0:r1, c * wb : (c + 1) * wb].astype(f32).astype(bf16)
            seen = (mm(part, spread).astype(jnp.int32) & bit) != 0
            x = x_ref[r0:r1, c * 8 * wb : (c + 1) * 8 * wb].astype(f32)
            x_ref[r0:r1, c * 8 * wb : (c + 1) * 8 * wb] = jnp.where(seen, x, MISSING).astype(bf16)

    present = jnp.asarray(PRESENT, bf16)

    def resid(c0, c1, fit):
        x = x_ref[:, c0:c1]
        return jnp.where(x < present, (x.astype(f32) - fit).astype(bf16), jnp.zeros_like(x))

    def g1(o, d):
        return rcopy(gsend.at[o], grecv.at[d], g1s.at[o], g1r.at[d], "prec", place(o))

    def g2(o, d):
        return rcopy(gtot.at[o], gtot.at[o], g2s.at[d], g2r.at[o], "prec", d)

    def p1(o, d):
        return rcopy(psend.at[o], precv.at[d], ps.at[o], pr.at[d], "prec", place(o))

    def t1(o, d):
        return rcopy(tb.at[o], tb.at[o], ts.at[d], tr.at[o], "prec", d)

    def each_owner(count, act):
        for j in range(count):
            o = lax.rem(me + j, count)

            @pl.when(place(o) != me)
            def _():
                act(o)

    def launch_u(update):
        gram = None
        for c in range(vchunks):
            c0, c1 = c * cw, (c + 1) * cw
            if update is not None:
                update(c)
            v = vt[:, c0:c1]
            gram = mm_nt(v, v) if gram is None else gram + mm_nt(v, v)
            if c == vchunks - 1:
                gsend[...] = pack_gram(gram).reshape(gsend.shape)
                each_owner(gowners, lambda o: g1(o, me).start())
            proj = mm_nt(resid(c0, c1, mm(u[...], v)), v)
            pacc[...] = proj if c == 0 else pacc[...] + proj
        both = jnp.concatenate([pacc[:half], pacc[half:]], axis=1)
        psend[...] = both.astype(bf16).reshape(psend.shape)
        each_owner(owners, lambda o: p1(o, me).start())

    def finish_u():
        @pl.when(gowns)
        def _():
            for d in others:
                g1(seat, d).wait_recv()
            grecv[me] = gsend[seat]
            total = grecv[0]
            for d in range(1, n):
                total = total + grecv[d]
            gtot[seat] = total
            for d in others:
                g2(seat, d).start()

        @pl.when(owns)
        def _():
            for d in others:
                p1(seat, d).wait_recv()
            total = psend[seat].astype(f32)
            for d in others:
                total = total + precv[d].astype(f32)
            tb[seat] = (total - ridge_value * ub[seat].astype(f32)).astype(bf16)
            for d in others:
                t1(seat, d).start()

        each_owner(gowners, lambda o: g2(o, me).wait_recv())
        ihi, ilo = split(spd_inverse(unpack_gram(gtot[...].reshape(k // 2, 2 * k))))
        none = jnp.zeros_like(ihi)
        rhs = jnp.concatenate(
            [jnp.concatenate(r, axis=1) for r in ((ihi, none), (none, ihi), (ilo, none), (none, ilo))],
            axis=0,
        )
        each_owner(owners, lambda o: t1(o, me).wait_recv())
        t = tb[...].reshape(half, 2 * k)
        step = mm(jnp.concatenate([t, t], axis=1), rhs)
        new = (ub[...].reshape(half, 2 * k).astype(f32) + step).astype(bf16)
        ub[...] = new.reshape(ub.shape)
        u[:half] = new[:, :k]
        u[half:] = new[:, k:]
        each_owner(gowners, lambda o: g1(o, me).wait_send())
        each_owner(owners, lambda o: p1(o, me).wait_send())

        @pl.when(gowns)
        def _():
            for d in others:
                g2(seat, d).wait_send()

        @pl.when(owns)
        def _():
            for d in others:
                t1(seat, d).wait_send()

    def launch_v(par):
        now = u[...]
        ut = mm_nt(eye, now).astype(bf16)
        for c in range(vchunks):
            c0, c1 = c * cw, (c + 1) * cw
            fit = mm(now, vt[:, c0:c1])
            pv[par, my, c] = mm(ut, resid(c0, c1, fit)).astype(bf16)
            for d in rothers:
                mine = pv.at[par, my, c]
                rcopy(mine, mine, pvs.at[d, c], pvr.at[par, my, c], "run", d).start()
            if c == 0:
                gu[par, my] = pack_gram(mm_nt(ut, ut))
                for d in rothers:
                    rcopy(gu.at[par, my], gu.at[par, my], gus.at[d], gur.at[par, my], "run", d).start()
        for d in rothers:
            rcopy(gu.at[par, my], gu.at[par, d], gus.at[d], gur.at[par, d], "run", d).wait()
        total = gu[par, 0]
        for d in range(1, nr):
            total = total + gu[par, d]
        ihi, ilo = split(spd_inverse(unpack_gram(total)))
        lhs = jnp.concatenate([ihi, ilo, ihi], axis=1)

        def update(c):
            c0, c1 = c * cw, (c + 1) * cw
            for d in rothers:
                rcopy(
                    pv.at[par, my, c], pv.at[par, d, c], pvs.at[d, c], pvr.at[par, d, c], "run", d
                ).wait()
            share = pv[par, 0, c].astype(f32)
            for d in range(1, nr):
                share = share + pv[par, d, c].astype(f32)
            old = vt[:, c0:c1].astype(f32)
            dhi, dlo = split(share - ridge_value * old)
            step = mm(lhs, jnp.concatenate([dhi, dhi, dlo], axis=0))
            vt[:, c0:c1] = (old + step).astype(bf16)

        return update

    pl.semaphore_wait(barrier, n - 1 + nr - 1)
    launch_u(None)

    def iteration(it, carry):
        finish_u()
        launch_u(launch_v(lax.rem(it, 2)))
        return carry

    lax.fori_loop(0, ITERS - 1, iteration, 0)
    finish_u()
    update = launch_v((ITERS - 1) % 2)
    for c in range(vchunks):
        c0, c1 = c * cw, (c + 1) * cw
        update(c)
        fit = mm(u[...], vt[:, c0:c1]).astype(bf16)
        x = x_ref[:, c0:c1]
        out_ref[:, c0:c1] = jnp.where(x < present, x, fit)


def local(n, nr, intensity, observed, run_factors, prec_factors):
    rows, cols = intensity.shape
    words = observed.shape[1]
    k = run_factors.shape[1]
    half = rows // 2
    owners = max(1, min(n // 2, half // 32))
    sp = half // owners
    gowners = max(1, min(owners, k // 16))
    gr = k // 2 // gowners
    vchunks = max(1, min(4, cols // 128))
    cw = cols // vchunks
    nb = max(1, rows // 128)
    dma = pltpu.SemaphoreType.DMA
    hbm = pl.BlockSpec(memory_space=pltpu.HBM)
    operands = (intensity, observed, run_factors.T, prec_factors.T)
    return pl.pallas_call(
        functools.partial(als_kernel, n, nr, owners, vchunks),
        out_shape=jax.ShapeDtypeStruct((rows, cols), bf16),
        in_specs=[hbm] * 4,
        out_specs=pl.BlockSpec(memory_space=pltpu.VMEM),
        scratch_shapes=[
            pltpu.VMEM((rows, cols), bf16),
            pltpu.VMEM((rows, words), jnp.int32),
            pltpu.VMEM((k, rows), bf16),
            pltpu.VMEM((rows, k), bf16),
            pltpu.VMEM((owners, sp, 2 * k), bf16),
            pltpu.VMEM((k, cols), bf16),
            pltpu.VMEM((rows, k), f32),
            pltpu.VMEM((gowners, gr, 2 * k), f32),
            pltpu.VMEM((n, gr, 2 * k), f32),
            pltpu.VMEM((gowners, gr, 2 * k), f32),
            pltpu.VMEM((owners, sp, 2 * k), bf16),
            pltpu.VMEM((n, sp, 2 * k), bf16),
            pltpu.VMEM((owners, sp, 2 * k), bf16),
            pltpu.VMEM((2, nr, k // 2, 2 * k), f32),
            pltpu.VMEM((2, nr, vchunks, k, cw), bf16),
            dma((nb,)), dma((nb,)), dma((2,)),
            dma((gowners,)), dma((n,)), dma((n,)), dma((gowners,)),
            dma((owners,)), dma((n,)), dma((n,)), dma((owners,)),
            dma((nr,)), dma((2, nr)), dma((nr, vchunks)), dma((2, nr, vchunks)),
        ],
        compiler_params=pltpu.CompilerParams(
            collective_id=0, has_side_effects=True, vmem_limit_bytes=VMEM_LIMIT
        ),
    )(*(pltpu.with_memory_space_constraint(a, pltpu.HBM) for a in operands))


def solution(mesh):
    n, nr = mesh.shape["prec"], mesh.shape["run"]
    return jax.shard_map(
        functools.partial(local, n, nr),
        mesh=mesh,
        in_specs=(P("run", "prec"), P("run", "prec"), P("run", None), P("prec", None)),
        out_specs=P("run", "prec"),
        check_vma=False,
    )
```

```python
import functools

import jax
import jax.numpy as jnp
from jax import lax
from jax.experimental import pallas as pl
from jax.experimental.pallas import tpu as pltpu
from jax.sharding import PartitionSpec as P

ITERS = 4
ridge_value = 16.0
f32 = jnp.float32
bf16 = jnp.bfloat16
MESH = pl.DeviceIdType.MESH
VMEM_LIMIT = 32 << 20
CHUNK_PARTS, CHUNK_CUTS = 4, (0, 1, 2, 3, 4)
MISSING = 2.0**100
PRESENT = 2.0**90


def mm(a, b):
    return lax.dot_general(a, b, (((1,), (0,)), ((), ())), preferred_element_type=f32)


def mm_nt(a, b):
    return lax.dot_general(a, b, (((1,), (1,)), ((), ())), preferred_element_type=f32)


def tree_sum(terms):
    while len(terms) > 1:
        terms = [sum(terms[i : i + 2]) for i in range(0, len(terms), 2)]
    return terms[0]


def spd_inverse(a):
    size = a.shape[0]
    wide = 2 * size
    eye = (
        lax.broadcasted_iota(jnp.int32, (size, size), 0)
        == lax.broadcasted_iota(jnp.int32, (size, size), 1)
    ).astype(f32)
    full = jnp.concatenate([a + ridge_value * eye, eye], axis=1)
    m = [full[i : i + 8] for i in range(0, size, 8)]
    row = lax.broadcasted_iota(jnp.int32, (8, wide), 0)

    def col(block, j):
        return jnp.broadcast_to(block[:, j : j + 1], (8, wide))

    for q in range(size // 8):
        pivot = m[q]
        cols = [col(pivot, 8 * q + j) for j in range(8)]
        for j in range(0, 8, 2):
            c0, c1 = cols[j], cols[j + 1]
            p00, p10, p01, p11 = c0[j : j + 1], c0[j + 1 : j + 2], c1[j : j + 1], c1[j + 1 : j + 2]
            inv = 1.0 / (p00 * p11 - p01 * p10)
            i00, i01, i10, i11 = p11 * inv, p01 * inv, p10 * inv, p00 * inv

            def eliminate(v):
                r0, r1 = v[j : j + 1], v[j + 1 : j + 2]
                x0, x1 = i00 * r0 - i01 * r1, i11 * r1 - i10 * r0
                rest = v - (c0 * x0 + c1 * x1)
                return jnp.where(row == j, x0, jnp.where(row == j + 1, x1, rest))

            cols = cols[: j + 2] + [eliminate(v) for v in cols[j + 2 :]]
            pivot = eliminate(pivot)
        m = [
            pivot
            if i == q
            else m[i] - tree_sum([col(m[i], 8 * q + j) * pivot[j : j + 1] for j in range(8)])
            for i in range(size // 8)
        ]
    return jnp.concatenate(m, axis=0)[:, size:]


def split(x):
    hi = x.astype(bf16)
    return hi, (x - hi.astype(f32)).astype(bf16)


def pack_gram(g):
    h = g.shape[0] // 2
    return jnp.concatenate([g[:h], g[h:]], axis=1)


def unpack_gram(x):
    h = x.shape[1] // 2
    return jnp.concatenate([x[:, :h], x[:, h:]], axis=0)


def als_kernel(
    n, nr, owners, bounds,
    x_hbm, w_hbm, ut0_hbm, vt0_hbm, out_ref,
    x_ref, w_ref, ut, u, ub, vt, pacc, gpart, gin, gall, gtot, psend, precv, tb, gu, pv,
    xs, wsem, vs, g1s, g1r, g2s, g2r, g3s, g3r, ps, pr, ts, tr, gus, gur, pvs, pvr,
):
    me = lax.axis_index("prec")
    my = lax.axis_index("run")
    k, cols = vt.shape
    rows = u.shape[0]
    half = rows // 2
    sp = half // owners
    vchunks = len(bounds) - 1
    base, stride = n // 4, n // 2 // owners
    others = [lax.rem(me + off, n) for off in range(1, n)]
    rothers = [lax.rem(my + off, nr) for off in range(1, nr)]
    offset = me - base
    seat = lax.div(offset, stride)
    owns = (offset >= 0) & (offset < owners * stride) & (offset == seat * stride)
    core, chip = lax.rem(me, 2), lax.div(me, 2)
    chips = [lax.rem(chip + off, n // 2) for off in range(1, n // 2)]

    nb = xs.shape[0]
    rb = rows // nb
    vload = pltpu.make_async_copy(vt0_hbm, vt, vs.at[0])
    uload = pltpu.make_async_copy(ut0_hbm, ut, vs.at[1])
    xload, wload = [], []
    for i in range(nb):
        span = slice(i * rb, (i + 1) * rb)
        wload.append(pltpu.make_async_copy(w_hbm.at[span], w_ref.at[span], wsem.at[i]))
        xload.append(pltpu.make_async_copy(x_hbm.at[span], x_ref.at[span], xs.at[i]))
    vload.start()
    uload.start()
    for i in range(nb):
        wload[i].start()
        xload[i].start()
    barrier = pltpu.get_barrier_semaphore()
    for d in others:
        pl.semaphore_signal(barrier, inc=1, device_id={"prec": d}, device_id_type=MESH)
    for d in rothers:
        pl.semaphore_signal(barrier, inc=1, device_id={"run": d}, device_id_type=MESH)

    def rcopy(src, dst, ss, rs, axis, d):
        return pltpu.make_async_remote_copy(
            src_ref=src, dst_ref=dst, send_sem=ss, recv_sem=rs,
            device_id={axis: d}, device_id_type=MESH,
        )

    def place(o):
        return base + o * stride

    vload.wait()
    uload.wait()
    start = jnp.transpose(ut[...].astype(f32))
    u[...] = start.astype(bf16)
    ub[...] = (
        jnp.concatenate([start[:half], start[half:]], axis=1).astype(bf16).reshape(ub.shape)
    )

    words = w_ref.shape[1]
    wb = min(128, words)
    spread = (
        lax.broadcasted_iota(jnp.int32, (wb, 8 * wb), 0)
        == lax.broadcasted_iota(jnp.int32, (wb, 8 * wb), 1) // 8
    ).astype(f32).astype(bf16)
    bit = jnp.left_shift(1, lax.broadcasted_iota(jnp.int32, (rb, 8 * wb), 1) & 7)
    for i in range(nb):
        r0, r1 = i * rb, (i + 1) * rb
        wload[i].wait()
        xload[i].wait()
        for c in range(words // wb):
            part = w_ref[r0:r1, c * wb : (c + 1) * wb].astype(f32).astype(bf16)
            seen = (mm(part, spread).astype(jnp.int32) & bit) != 0
            x = x_ref[r0:r1, c * 8 * wb : (c + 1) * 8 * wb].astype(f32)
            x_ref[r0:r1, c * 8 * wb : (c + 1) * 8 * wb] = jnp.where(seen, x, MISSING).astype(bf16)

    present = jnp.asarray(PRESENT, bf16)

    def resid(c0, c1, fit):
        x = x_ref[:, c0:c1]
        return jnp.where(x < present, (x.astype(f32) - fit).astype(bf16), jnp.zeros_like(x))

    g1 = rcopy(gpart.at[1 - core], gin, g1s, g1r, "prec", me + 1 - 2 * core)

    g3 = rcopy(gtot.at[core], gtot.at[core], g3s, g3r, "prec", me + 1 - 2 * core)
    g3_in = rcopy(gtot.at[core], gtot.at[1 - core], g3s, g3r, "prec", me + 1 - 2 * core)

    def g2(par, o, c):
        return rcopy(gall.at[par, o], gall.at[par, o], g2s.at[c], g2r.at[par, o], "prec", 2 * c + core)

    def p1(o, d):
        return rcopy(psend.at[o], precv.at[d], ps.at[o], pr.at[d], "prec", place(o))

    def t1(o, d):
        return rcopy(tb.at[o], tb.at[o], ts.at[d], tr.at[o], "prec", d)

    def each_owner(count, act):
        for o in range(count):

            @pl.when(place(o) != me)
            def _():
                act(o)

    def far_first(act):
        for j in range(n):
            d = jnp.where(me < n // 2, n - 1 - j, j)

            @pl.when(d != me)
            def _():
                act(d)

    def launch_u(update, par):
        gram = None
        for c in range(vchunks):
            c0, c1 = bounds[c], bounds[c + 1]
            if update is not None:
                update(c)
            v = vt[:, c0:c1]
            gram = mm_nt(v, v) if gram is None else gram + mm_nt(v, v)
            res = resid(c0, c1, mm(u[...], v))
            for h in range(2):
                proj = mm_nt(res[h * half : (h + 1) * half], v)
                pacc[h] = proj if c == 0 else pacc[h] + proj
        both = jnp.concatenate([pacc[0], pacc[1]], axis=1)
        psend[...] = both.astype(bf16).reshape(psend.shape)
        gpart[...] = pack_gram(gram).reshape(gpart.shape)
        each_owner(owners, lambda o: p1(o, me).start())
        g1.start()

    def finish_u(par):
        g1.wait_recv()
        gall[par, chip] = gpart[core] + gin[...]
        for c in chips:
            g2(par, chip, c).start()

        @pl.when(owns)
        def _():
            for d in others:
                p1(seat, d).wait_recv()
            total = psend[seat].astype(f32)
            for d in others:
                total = total + precv[d].astype(f32)
            tb[seat] = (total - ridge_value * ub[seat].astype(f32)).astype(bf16)
            far_first(lambda d: t1(seat, d).start())

        for c in chips:
            g2(par, c, chip).wait_recv()
        total = gall[par, 0]
        for c in range(1, n // 2):
            total = total + gall[par, c]
        gtot[core] = total
        g3.start()
        g3_in.wait_recv()
        ihi, ilo = split(spd_inverse(unpack_gram(gtot[...].reshape(k // 2, 2 * k))))
        none = jnp.zeros_like(ihi)
        rhs = jnp.concatenate(
            [jnp.concatenate(r, axis=1) for r in ((ihi, none), (none, ihi), (ilo, none), (none, ilo))],
            axis=0,
        )
        lhs = jnp.concatenate(
            [jnp.concatenate(r, axis=1) for r in ((ihi, none, ilo, none), (none, ihi, none, ilo))], axis=0
        )
        each_owner(owners, lambda o: t1(o, me).wait_recv())
        t = tb[...].reshape(half, 2 * k)
        twice = jnp.concatenate([t, t], axis=1)
        step = mm(twice, rhs)
        step_t = mm_nt(lhs, twice)
        step_t = jnp.concatenate([step_t[:k], step_t[k:]], axis=1)
        ut[...] = (ut[...].astype(f32) + step_t).astype(bf16)
        new = (ub[...].reshape(half, 2 * k).astype(f32) + step).astype(bf16)
        ub[...] = new.reshape(ub.shape)
        u[:half] = new[:, :k]
        u[half:] = new[:, k:]

    def sent_u(par):
        g1.wait_send()
        for c in chips:
            g2(par, chip, c).wait_send()
        g3.wait_send()
        each_owner(owners, lambda o: p1(o, me).wait_send())

        @pl.when(owns)
        def _():
            for d in others:
                t1(seat, d).wait_send()

    def launch_v(par):
        now = u[...]
        now_t = ut[...]
        gu[par, my] = pack_gram(mm_nt(now_t, now_t))
        for d in rothers:
            rcopy(gu.at[par, my], gu.at[par, my], gus.at[d], gur.at[par, my], "run", d).start()
        for c in range(vchunks):
            c0, c1 = bounds[c], bounds[c + 1]
            fit = mm(now, vt[:, c0:c1])
            pv[c][par, my] = mm(now_t, resid(c0, c1, fit)).astype(bf16)
            for d in rothers:
                mine = pv[c].at[par, my]
                rcopy(mine, mine, pvs.at[d, c], pvr.at[par, my, c], "run", d).start()
        sent_u(par)
        for d in rothers:
            rcopy(gu.at[par, my], gu.at[par, d], gus.at[d], gur.at[par, d], "run", d).wait()
        total = gu[par, 0]
        for d in range(1, nr):
            total = total + gu[par, d]
        ihi, ilo = split(spd_inverse(unpack_gram(total)))
        lhs = jnp.concatenate([ihi, ilo, ihi], axis=1)

        def update(c):
            c0, c1 = bounds[c], bounds[c + 1]
            for d in rothers:
                rcopy(
                    pv[c].at[par, my], pv[c].at[par, d], pvs.at[d, c], pvr.at[par, d, c], "run", d
                ).wait()
            share = pv[c][par, 0].astype(f32)
            for d in range(1, nr):
                share = share + pv[c][par, d].astype(f32)
            old = vt[:, c0:c1].astype(f32)
            dhi, dlo = split(share - ridge_value * old)
            step = mm(lhs, jnp.concatenate([dhi, dhi, dlo], axis=0))
            vt[:, c0:c1] = (old + step).astype(bf16)

        return update

    pl.semaphore_wait(barrier, n - 1 + nr - 1)
    launch_u(None, 0)

    def iteration(it, carry):
        par = lax.rem(it, 2)
        finish_u(par)
        launch_u(launch_v(par), 1 - par)
        return carry

    lax.fori_loop(0, ITERS - 1, iteration, 0)
    finish_u((ITERS - 1) % 2)
    update = launch_v((ITERS - 1) % 2)
    for c in range(vchunks):
        c0, c1 = bounds[c], bounds[c + 1]
        update(c)
        fit = mm(u[...], vt[:, c0:c1]).astype(bf16)
        x = x_ref[:, c0:c1]
        out_ref[:, c0:c1] = jnp.where(x < present, x, fit)


def chunk_bounds(cols):
    unit = cols // CHUNK_PARTS
    if unit % 128:
        return (0, cols)
    return tuple(unit * c for c in CHUNK_CUTS)


def local(n, nr, intensity, observed, run_factors, prec_factors):
    rows, cols = intensity.shape
    words = observed.shape[1]
    k = run_factors.shape[1]
    half = rows // 2
    owners = max(1, min(n // 2, half // 32))
    sp = half // owners
    bounds = chunk_bounds(cols)
    vchunks = len(bounds) - 1
    nb = max(1, rows // 128)
    dma = pltpu.SemaphoreType.DMA
    hbm = pl.BlockSpec(memory_space=pltpu.HBM)
    operands = (intensity, observed, run_factors.T, prec_factors.T)
    return pl.pallas_call(
        functools.partial(als_kernel, n, nr, owners, bounds),
        out_shape=jax.ShapeDtypeStruct((rows, cols), bf16),
        in_specs=[hbm] * 4,
        out_specs=pl.BlockSpec(memory_space=pltpu.VMEM),
        scratch_shapes=[
            pltpu.VMEM((rows, cols), bf16),
            pltpu.VMEM((rows, words), jnp.int32),
            pltpu.VMEM((k, rows), bf16),
            pltpu.VMEM((rows, k), bf16),
            pltpu.VMEM((owners, sp, 2 * k), bf16),
            pltpu.VMEM((k, cols), bf16),
            pltpu.VMEM((2, half, k), f32),
            pltpu.VMEM((2, k // 4, 2 * k), f32),
            pltpu.VMEM((k // 4, 2 * k), f32),
            pltpu.VMEM((2, n // 2, k // 4, 2 * k), f32),
            pltpu.VMEM((2, k // 4, 2 * k), f32),
            pltpu.VMEM((owners, sp, 2 * k), bf16),
            pltpu.VMEM((n, sp, 2 * k), bf16),
            pltpu.VMEM((owners, sp, 2 * k), bf16),
            pltpu.VMEM((2, nr, k // 2, 2 * k), f32),
            [pltpu.VMEM((2, nr, k, b - a), bf16) for a, b in zip(bounds, bounds[1:])],
            dma((nb,)), dma((nb,)), dma((2,)),
            dma(()), dma(()), dma((n // 2,)), dma((2, n // 2)), dma(()), dma(()),
            dma((owners,)), dma((n,)), dma((n,)), dma((owners,)),
            dma((nr,)), dma((2, nr)), dma((nr, vchunks)), dma((2, nr, vchunks)),
        ],
        compiler_params=pltpu.CompilerParams(
            collective_id=0, has_side_effects=True, vmem_limit_bytes=VMEM_LIMIT
        ),
    )(*(pltpu.with_memory_space_constraint(a, pltpu.HBM) for a in operands))


def solution(mesh):
    n, nr = mesh.shape["prec"], mesh.shape["run"]
    return jax.shard_map(
        functools.partial(local, n, nr),
        mesh=mesh,
        in_specs=(P("run", "prec"), P("run", "prec"), P("run", None), P("prec", None)),
        out_specs=P("run", "prec"),
        check_vma=False,
    )
```

```python
import functools

import jax
import jax.numpy as jnp
from jax import lax
from jax.experimental import pallas as pl
from jax.experimental.pallas import tpu as pltpu
from jax.sharding import PartitionSpec as P

ITERS = 4
ridge_value = 16.0
f32 = jnp.float32
bf16 = jnp.bfloat16
MESH = pl.DeviceIdType.MESH
VMEM_LIMIT = 32 << 20
CHUNK_PARTS, CHUNK_CUTS = 4, (0, 1, 2, 3, 4)
MISSING = 2.0**100
PRESENT = 2.0**90
SCALE = 2.0**-60


def mm(a, b):
    return lax.dot_general(a, b, (((1,), (0,)), ((), ())), preferred_element_type=f32)


def mm_nt(a, b):
    return lax.dot_general(a, b, (((1,), (1,)), ((), ())), preferred_element_type=f32)


def tree_sum(terms):
    while len(terms) > 1:
        terms = [sum(terms[i : i + 2]) for i in range(0, len(terms), 2)]
    return terms[0]


def spd_inverse(a):
    size = a.shape[0]
    wide = 2 * size
    eye = (
        lax.broadcasted_iota(jnp.int32, (size, size), 0)
        == lax.broadcasted_iota(jnp.int32, (size, size), 1)
    ).astype(f32)
    full = jnp.concatenate([(a + ridge_value * eye) * SCALE, eye], axis=1)
    m = [full[i : i + 8] for i in range(0, size, 8)]
    row = lax.broadcasted_iota(jnp.int32, (8, wide), 0)

    def col(block, j):
        return jnp.broadcast_to(block[:, j : j + 1], (8, wide))

    for q in range(size // 8):
        pivot = m[q]
        cols = [col(pivot, 8 * q + j) for j in range(8)]
        for j in range(0, 8, 2):
            c0, c1 = cols[j], cols[j + 1]
            p00, p10, p01, p11 = c0[j : j + 1], c0[j + 1 : j + 2], c1[j : j + 1], c1[j + 1 : j + 2]
            inv = 1.0 / (p00 * p11 - p01 * p10)
            i00, i01, i10, i11 = p11 * inv, p01 * inv, p10 * inv, p00 * inv

            def eliminate(v):
                r0, r1 = v[j : j + 1], v[j + 1 : j + 2]
                x0, x1 = i00 * r0 - i01 * r1, i11 * r1 - i10 * r0
                rest = v - (c0 * x0 + c1 * x1)
                return jnp.where(row == j, x0, jnp.where(row == j + 1, x1, rest))

            cols = cols[: j + 2] + [eliminate(v) for v in cols[j + 2 :]]
            pivot = eliminate(pivot)
        m = [
            pivot
            if i == q
            else m[i] - tree_sum([col(m[i], 8 * q + j) * pivot[j : j + 1] for j in range(8)])
            for i in range(size // 8)
        ]
    return jnp.concatenate(m, axis=0)[:, size:] * SCALE


def split(x):
    hi = x.astype(bf16)
    return hi, (x - hi.astype(f32)).astype(bf16)


def pack_gram(g):
    h = g.shape[0] // 2
    return jnp.concatenate([g[:h], g[h:]], axis=1)


def unpack_gram(x):
    h = x.shape[1] // 2
    return jnp.concatenate([x[:, :h], x[:, h:]], axis=0)


def als_kernel(
    n, nr, owners, bounds,
    x_hbm, w_hbm, ut0_hbm, vt0_hbm, out_ref,
    x_ref, w_ref, ut, u, ub, vt, pacc, gpart, gin, gall, gtot, psend, precv, tb, gu, pv,
    xs, wsem, vs, g1s, g1r, g2s, g2r, g3s, g3r, ps, pr, ts, tr, gus, gur, pvs, pvr,
):
    me = lax.axis_index("prec")
    my = lax.axis_index("run")
    k, cols = vt.shape
    rows = u.shape[0]
    half = rows // 2
    sp = half // owners
    vchunks = len(bounds) - 1
    base, stride = n // 4, n // 2 // owners
    others = [lax.rem(me + off, n) for off in range(1, n)]
    rothers = [lax.rem(my + off, nr) for off in range(1, nr)]
    offset = me - base
    seat = lax.div(offset, stride)
    owns = (offset >= 0) & (offset < owners * stride) & (offset == seat * stride)
    core, chip = lax.rem(me, 2), lax.div(me, 2)
    chips = [lax.rem(chip + off, n // 2) for off in range(1, n // 2)]

    nb = xs.shape[0]
    rb = rows // nb
    vload = pltpu.make_async_copy(vt0_hbm, vt, vs.at[0])
    uload = pltpu.make_async_copy(ut0_hbm, ut, vs.at[1])
    xload, wload = [], []
    for i in range(nb):
        span = slice(i * rb, (i + 1) * rb)
        wload.append(pltpu.make_async_copy(w_hbm.at[span], w_ref.at[span], wsem.at[i]))
        xload.append(pltpu.make_async_copy(x_hbm.at[span], x_ref.at[span], xs.at[i]))
    vload.start()
    uload.start()
    for i in range(nb):
        wload[i].start()
        xload[i].start()
    barrier = pltpu.get_barrier_semaphore()
    for d in others:
        pl.semaphore_signal(barrier, inc=1, device_id={"prec": d}, device_id_type=MESH)
    for d in rothers:
        pl.semaphore_signal(barrier, inc=1, device_id={"run": d}, device_id_type=MESH)

    def rcopy(src, dst, ss, rs, axis, d):
        return pltpu.make_async_remote_copy(
            src_ref=src, dst_ref=dst, send_sem=ss, recv_sem=rs,
            device_id={axis: d}, device_id_type=MESH,
        )

    def place(o):
        return base + o * stride

    vload.wait()
    uload.wait()
    start = jnp.transpose(ut[...].astype(f32))
    u[...] = start.astype(bf16)
    ub[...] = (
        jnp.concatenate([start[:half], start[half:]], axis=1).astype(bf16).reshape(ub.shape)
    )

    words = w_ref.shape[1]
    wb = min(128, words)
    spread = (
        lax.broadcasted_iota(jnp.int32, (wb, 8 * wb), 0)
        == lax.broadcasted_iota(jnp.int32, (wb, 8 * wb), 1) // 8
    ).astype(f32).astype(bf16)
    bit = jnp.left_shift(1, lax.broadcasted_iota(jnp.int32, (rb, 8 * wb), 1) & 7)
    for i in range(nb):
        r0, r1 = i * rb, (i + 1) * rb
        wload[i].wait()
        xload[i].wait()
        for c in range(words // wb):
            part = w_ref[r0:r1, c * wb : (c + 1) * wb].astype(f32).astype(bf16)
            seen = (mm(part, spread).astype(jnp.int32) & bit) != 0
            x = x_ref[r0:r1, c * 8 * wb : (c + 1) * 8 * wb].astype(f32)
            x_ref[r0:r1, c * 8 * wb : (c + 1) * 8 * wb] = jnp.where(seen, x, MISSING).astype(bf16)

    present = jnp.asarray(PRESENT, bf16)

    def resid(c0, c1, fit):
        x = x_ref[:, c0:c1]
        return jnp.where(x < present, (x.astype(f32) - fit).astype(bf16), jnp.zeros_like(x))

    g1 = rcopy(gpart.at[1 - core], gin, g1s, g1r, "prec", me + 1 - 2 * core)

    g3 = rcopy(gtot.at[core], gtot.at[core], g3s, g3r, "prec", me + 1 - 2 * core)
    g3_in = rcopy(gtot.at[core], gtot.at[1 - core], g3s, g3r, "prec", me + 1 - 2 * core)

    def g2(par, o, c):
        return rcopy(gall.at[par, o], gall.at[par, o], g2s.at[c], g2r.at[par, o], "prec", 2 * c + core)

    def p1(o, d):
        return rcopy(psend.at[o], precv.at[d], ps.at[o], pr.at[d], "prec", place(o))

    def t1(o, d):
        return rcopy(tb.at[o], tb.at[o], ts.at[d], tr.at[o], "prec", d)

    def each_owner(count, act):
        for j in range(count - 1):
            act(j + (owns & (seat <= j)).astype(jnp.int32))

        @pl.when(jnp.logical_not(owns))
        def _():
            act(count - 1)

    def far_first(act):
        for j in range(n - 1):
            down = n - 1 - j
            act(jnp.where(me < n // 2, down - (down <= me).astype(jnp.int32), j + (j >= me).astype(jnp.int32)))

    def launch_u(update, par):
        gram = None
        for c in range(vchunks):
            c0, c1 = bounds[c], bounds[c + 1]
            if update is not None:
                update(c)
            v = vt[:, c0:c1]
            gram = mm_nt(v, v) if gram is None else gram + mm_nt(v, v)
            res = resid(c0, c1, mm(u[...], v))
            for h in range(2):
                proj = mm_nt(res[h * half : (h + 1) * half], v)
                pacc[h] = proj if c == 0 else pacc[h] + proj
        both = jnp.concatenate([pacc[0], pacc[1]], axis=1)
        psend[...] = both.astype(bf16).reshape(psend.shape)
        gpart[...] = pack_gram(gram).reshape(gpart.shape)
        each_owner(owners, lambda o: p1(o, me).start())
        g1.start()

    def finish_u(par):
        g1.wait_recv()
        gall[par, chip] = gpart[core] + gin[...]
        for c in chips:
            g2(par, chip, c).start()

        @pl.when(owns)
        def _():
            for d in others:
                p1(seat, d).wait_recv()
            total = psend[seat].astype(f32)
            for d in others:
                total = total + precv[d].astype(f32)
            tb[seat] = (total - ridge_value * ub[seat].astype(f32)).astype(bf16)
            far_first(lambda d: t1(seat, d).start())

        for c in chips:
            g2(par, c, chip).wait_recv()
        total = gall[par, 0]
        for c in range(1, n // 2):
            total = total + gall[par, c]
        gtot[core] = total
        g3.start()
        g3_in.wait_recv()
        ihi, ilo = split(spd_inverse(unpack_gram(gtot[...].reshape(k // 2, 2 * k))))
        none = jnp.zeros_like(ihi)
        rhs = jnp.concatenate(
            [jnp.concatenate(r, axis=1) for r in ((ihi, none), (none, ihi), (ilo, none), (none, ilo))],
            axis=0,
        )
        lhs = jnp.concatenate(
            [jnp.concatenate(r, axis=1) for r in ((ihi, none, ilo, none), (none, ihi, none, ilo))], axis=0
        )
        each_owner(owners, lambda o: t1(o, me).wait_recv())
        t = tb[...].reshape(half, 2 * k)
        twice = jnp.concatenate([t, t], axis=1)
        step = mm(twice, rhs)
        step_t = mm_nt(lhs, twice)
        step_t = jnp.concatenate([step_t[:k], step_t[k:]], axis=1)
        ut[...] = (ut[...].astype(f32) + step_t).astype(bf16)
        new = (ub[...].reshape(half, 2 * k).astype(f32) + step).astype(bf16)
        ub[...] = new.reshape(ub.shape)
        u[:half] = new[:, :k]
        u[half:] = new[:, k:]

    def sent_u(par):
        g1.wait_send()
        for c in chips:
            g2(par, chip, c).wait_send()
        g3.wait_send()
        each_owner(owners, lambda o: p1(o, me).wait_send())

        @pl.when(owns)
        def _():
            for d in others:
                t1(seat, d).wait_send()

    def launch_v(par):
        now = u[...]
        now_t = ut[...]
        gu[par, my] = pack_gram(mm_nt(now_t, now_t))
        for d in rothers:
            rcopy(gu.at[par, my], gu.at[par, my], gus.at[d], gur.at[par, my], "run", d).start()
        for c in range(vchunks):
            c0, c1 = bounds[c], bounds[c + 1]
            fit = mm(now, vt[:, c0:c1])
            pv[c][par, my] = mm(now_t, resid(c0, c1, fit)).astype(bf16)
            for d in rothers:
                mine = pv[c].at[par, my]
                rcopy(mine, mine, pvs.at[d, c], pvr.at[par, my, c], "run", d).start()
        sent_u(par)
        for d in rothers:
            rcopy(gu.at[par, my], gu.at[par, d], gus.at[d], gur.at[par, d], "run", d).wait()
        total = gu[par, 0]
        for d in range(1, nr):
            total = total + gu[par, d]
        ihi, ilo = split(spd_inverse(unpack_gram(total)))
        lhs = jnp.concatenate([ihi, ilo, ihi], axis=1)

        def update(c):
            c0, c1 = bounds[c], bounds[c + 1]
            for d in rothers:
                rcopy(
                    pv[c].at[par, my], pv[c].at[par, d], pvs.at[d, c], pvr.at[par, d, c], "run", d
                ).wait()
            share = pv[c][par, 0].astype(f32)
            for d in range(1, nr):
                share = share + pv[c][par, d].astype(f32)
            old = vt[:, c0:c1].astype(f32)
            dhi, dlo = split(share - ridge_value * old)
            step = mm(lhs, jnp.concatenate([dhi, dhi, dlo], axis=0))
            vt[:, c0:c1] = (old + step).astype(bf16)

        return update

    pl.semaphore_wait(barrier, n - 1 + nr - 1)
    launch_u(None, 0)

    def iteration(it, carry):
        par = lax.rem(it, 2)
        finish_u(par)
        launch_u(launch_v(par), 1 - par)
        return carry

    lax.fori_loop(0, ITERS - 1, iteration, 0)
    finish_u((ITERS - 1) % 2)
    update = launch_v((ITERS - 1) % 2)
    for c in range(vchunks):
        c0, c1 = bounds[c], bounds[c + 1]
        update(c)
        fit = mm(u[...], vt[:, c0:c1]).astype(bf16)
        x = x_ref[:, c0:c1]
        out_ref[:, c0:c1] = jnp.where(x < present, x, fit)


def chunk_bounds(cols):
    unit = cols // CHUNK_PARTS
    if unit % 128:
        return (0, cols)
    return tuple(unit * c for c in CHUNK_CUTS)


def local(n, nr, intensity, observed, run_factors, prec_factors):
    rows, cols = intensity.shape
    words = observed.shape[1]
    k = run_factors.shape[1]
    half = rows // 2
    owners = max(1, min(n // 2, half // 32))
    sp = half // owners
    bounds = chunk_bounds(cols)
    vchunks = len(bounds) - 1
    nb = max(1, rows // 128)
    dma = pltpu.SemaphoreType.DMA
    hbm = pl.BlockSpec(memory_space=pltpu.HBM)
    operands = (intensity, observed, run_factors.T, prec_factors.T)
    return pl.pallas_call(
        functools.partial(als_kernel, n, nr, owners, bounds),
        out_shape=jax.ShapeDtypeStruct((rows, cols), bf16),
        in_specs=[hbm] * 4,
        out_specs=pl.BlockSpec(memory_space=pltpu.VMEM),
        scratch_shapes=[
            pltpu.VMEM((rows, cols), bf16),
            pltpu.VMEM((rows, words), jnp.int32),
            pltpu.VMEM((k, rows), bf16),
            pltpu.VMEM((rows, k), bf16),
            pltpu.VMEM((owners, sp, 2 * k), bf16),
            pltpu.VMEM((k, cols), bf16),
            pltpu.VMEM((2, half, k), f32),
            pltpu.VMEM((2, k // 4, 2 * k), f32),
            pltpu.VMEM((k // 4, 2 * k), f32),
            pltpu.VMEM((2, n // 2, k // 4, 2 * k), f32),
            pltpu.VMEM((2, k // 4, 2 * k), f32),
            pltpu.VMEM((owners, sp, 2 * k), bf16),
            pltpu.VMEM((n, sp, 2 * k), bf16),
            pltpu.VMEM((owners, sp, 2 * k), bf16),
            pltpu.VMEM((2, nr, k // 2, 2 * k), f32),
            [pltpu.VMEM((2, nr, k, b - a), bf16) for a, b in zip(bounds, bounds[1:])],
            dma((nb,)), dma((nb,)), dma((2,)),
            dma(()), dma(()), dma((n // 2,)), dma((2, n // 2)), dma(()), dma(()),
            dma((owners,)), dma((n,)), dma((n,)), dma((owners,)),
            dma((nr,)), dma((2, nr)), dma((nr, vchunks)), dma((2, nr, vchunks)),
        ],
        compiler_params=pltpu.CompilerParams(
            collective_id=0, has_side_effects=True, vmem_limit_bytes=VMEM_LIMIT,
        ),
    )(*(pltpu.with_memory_space_constraint(a, pltpu.HBM) for a in operands))


def solution(mesh):
    n, nr = mesh.shape["prec"], mesh.shape["run"]
    return jax.shard_map(
        functools.partial(local, n, nr),
        mesh=mesh,
        in_specs=(P("run", "prec"), P("run", "prec"), P("run", None), P("prec", None)),
        out_specs=P("run", "prec"),
        check_vma=False,
    )
```

```python
import functools

import jax
import jax.numpy as jnp
from jax import lax
from jax.experimental import pallas as pl
from jax.experimental.pallas import tpu as pltpu
from jax.sharding import PartitionSpec as P

ITERS = 4
ridge_value = 16.0
f32 = jnp.float32
bf16 = jnp.bfloat16
MESH = pl.DeviceIdType.MESH
VMEM_LIMIT = 32 << 20
CHUNK_PARTS, CHUNK_CUTS = 4, (0, 1, 2, 3, 4)
MISSING = 2.0**100
PRESENT = 2.0**90
SCALE = 2.0**-60


def mm(a, b):
    return lax.dot_general(a, b, (((1,), (0,)), ((), ())), preferred_element_type=f32)


def mm_nt(a, b):
    return lax.dot_general(a, b, (((1,), (1,)), ((), ())), preferred_element_type=f32)


def tree_sum(terms):
    while len(terms) > 1:
        terms = [sum(terms[i : i + 2]) for i in range(0, len(terms), 2)]
    return terms[0]


def spd_inverse(a):
    size = a.shape[0]
    wide = 2 * size
    eye = (
        lax.broadcasted_iota(jnp.int32, (size, size), 0)
        == lax.broadcasted_iota(jnp.int32, (size, size), 1)
    ).astype(f32)
    full = jnp.concatenate([(a + ridge_value * eye) * SCALE, eye], axis=1)
    m = [full[i : i + 8] for i in range(0, size, 8)]
    row = lax.broadcasted_iota(jnp.int32, (8, wide), 0)

    def col(block, j):
        return jnp.broadcast_to(block[:, j : j + 1], (8, wide))

    for q in range(size // 8):
        pivot = m[q]
        cols = [col(pivot, 8 * q + j) for j in range(8)]
        for j in range(0, 8, 2):
            c0, c1 = cols[j], cols[j + 1]
            p00, p10, p01, p11 = c0[j : j + 1], c0[j + 1 : j + 2], c1[j : j + 1], c1[j + 1 : j + 2]
            inv = 1.0 / (p00 * p11 - p01 * p10)
            i00, i01, i10, i11 = p11 * inv, p01 * inv, p10 * inv, p00 * inv

            def eliminate(v):
                r0, r1 = v[j : j + 1], v[j + 1 : j + 2]
                x0, x1 = i00 * r0 - i01 * r1, i11 * r1 - i10 * r0
                rest = v - (c0 * x0 + c1 * x1)
                return jnp.where(row == j, x0, jnp.where(row == j + 1, x1, rest))

            cols = cols[: j + 2] + [eliminate(v) for v in cols[j + 2 :]]
            pivot = eliminate(pivot)
        m = [
            pivot
            if i == q
            else m[i] - tree_sum([col(m[i], 8 * q + j) * pivot[j : j + 1] for j in range(8)])
            for i in range(size // 8)
        ]
    return jnp.concatenate(m, axis=0)[:, size:] * SCALE


def split(x):
    hi = x.astype(bf16)
    return hi, (x - hi.astype(f32)).astype(bf16)


def pack_gram(g):
    h = g.shape[0] // 2
    return jnp.concatenate([g[:h], g[h:]], axis=1)


def unpack_gram(x):
    h = x.shape[1] // 2
    return jnp.concatenate([x[:, :h], x[:, h:]], axis=0)


def als_kernel(
    n, nr, owners, bounds,
    x_hbm, w_hbm, ut0_hbm, vt0_hbm, out_ref,
    x_ref, w_ref, ut, u, ub, vt, pacc, gpart, gin, gall, gtot, psend, precv, tb, gu, pv,
    xs, wsem, vs, g1s, g1r, g2s, g2r, g3s, g3r, ps, pr, ts, tr, gus, gur, pvs, pvr,
):
    me = lax.axis_index("prec")
    my = lax.axis_index("run")
    k, cols = vt.shape
    rows = u.shape[0]
    half = rows // 2
    sp = half // owners
    vchunks = len(bounds) - 1
    base, stride = n // 4, n // 2 // owners
    others = [lax.rem(me + off, n) for off in range(1, n)]
    rothers = [lax.rem(my + off, nr) for off in range(1, nr)]
    offset = me - base
    seat = lax.div(offset, stride)
    owns = (offset >= 0) & (offset < owners * stride) & (offset == seat * stride)
    core, chip = lax.rem(me, 2), lax.div(me, 2)
    chips = [lax.rem(chip + off, n // 2) for off in range(1, n // 2)]

    nb = xs.shape[0]
    rb = rows // nb
    vload = pltpu.make_async_copy(vt0_hbm, vt, vs.at[0])
    uload = pltpu.make_async_copy(ut0_hbm, ut, vs.at[1])
    xload, wload = [], []
    for i in range(nb):
        span = slice(i * rb, (i + 1) * rb)
        wload.append(pltpu.make_async_copy(w_hbm.at[span], w_ref.at[span], wsem.at[i]))
        xload.append(pltpu.make_async_copy(x_hbm.at[span], x_ref.at[span], xs.at[i]))
    vload.start()
    uload.start()
    for i in range(nb):
        wload[i].start()
        xload[i].start()
    barrier = pltpu.get_barrier_semaphore()
    for d in others:
        pl.semaphore_signal(barrier, inc=1, device_id={"prec": d}, device_id_type=MESH)
    for d in rothers:
        pl.semaphore_signal(barrier, inc=1, device_id={"run": d}, device_id_type=MESH)

    def rcopy(src, dst, ss, rs, axis, d):
        return pltpu.make_async_remote_copy(
            src_ref=src, dst_ref=dst, send_sem=ss, recv_sem=rs,
            device_id={axis: d}, device_id_type=MESH,
        )

    def place(o):
        return base + o * stride

    vload.wait()
    uload.wait()
    start = jnp.transpose(ut[...].astype(f32))
    u[...] = start.astype(bf16)
    ub[...] = (
        jnp.concatenate([start[:half], start[half:]], axis=1).astype(bf16).reshape(ub.shape)
    )

    words = w_ref.shape[1]
    wb = min(128, words)
    spread = (
        lax.broadcasted_iota(jnp.int32, (wb, 8 * wb), 0)
        == lax.broadcasted_iota(jnp.int32, (wb, 8 * wb), 1) // 8
    ).astype(f32).astype(bf16)
    bit = jnp.left_shift(1, lax.broadcasted_iota(jnp.int32, (rb, 8 * wb), 1) & 7)
    for i in range(nb):
        r0, r1 = i * rb, (i + 1) * rb
        wload[i].wait()
        xload[i].wait()
        for c in range(words // wb):
            part = w_ref[r0:r1, c * wb : (c + 1) * wb].astype(f32).astype(bf16)
            seen = (mm(part, spread).astype(jnp.int32) & bit) != 0
            x = x_ref[r0:r1, c * 8 * wb : (c + 1) * 8 * wb].astype(f32)
            x_ref[r0:r1, c * 8 * wb : (c + 1) * 8 * wb] = jnp.where(seen, x, MISSING).astype(bf16)

    present = jnp.asarray(PRESENT, bf16)

    def resid(c0, c1, fit):
        x = x_ref[:, c0:c1]
        return jnp.where(x < present, (x.astype(f32) - fit).astype(bf16), jnp.zeros_like(x))

    g1 = rcopy(gpart.at[1 - core], gin, g1s, g1r, "prec", me + 1 - 2 * core)

    g3 = rcopy(gtot.at[core], gtot.at[core], g3s, g3r, "prec", me + 1 - 2 * core)
    g3_in = rcopy(gtot.at[core], gtot.at[1 - core], g3s, g3r, "prec", me + 1 - 2 * core)

    def g2(par, o, c):
        return rcopy(gall.at[par, o], gall.at[par, o], g2s.at[c], g2r.at[par, o], "prec", 2 * c + core)

    def p1(o, d):
        return rcopy(psend.at[o], precv.at[d], ps.at[o], pr.at[d], "prec", place(o))

    def t1(o, d):
        return rcopy(tb.at[o], tb.at[o], ts.at[d], tr.at[o], "prec", d)

    def each_owner(count, act):
        def at(j):
            return jnp.where(me < n // 2, count - 1 - j, j)

        spot = at(seat)
        for j in range(count - 1):
            act(at(j + (owns & (spot <= j)).astype(jnp.int32)))

        @pl.when(jnp.logical_not(owns))
        def _():
            act(at(count - 1))

    def far_first(act):
        for j in range(n - 1):
            down = n - 1 - j
            act(jnp.where(me < n // 2, down - (down <= me).astype(jnp.int32), j + (j >= me).astype(jnp.int32)))

    def launch_u(update, par):
        gram = None
        for c in range(vchunks):
            c0, c1 = bounds[c], bounds[c + 1]
            if update is not None:
                update(c)
            v = vt[:, c0:c1]
            gram = mm_nt(v, v) if gram is None else gram + mm_nt(v, v)
            res = resid(c0, c1, mm(u[...], v))
            for h in range(2):
                proj = mm_nt(res[h * half : (h + 1) * half], v)
                pacc[h] = proj if c == 0 else pacc[h] + proj
        both = jnp.concatenate([pacc[0], pacc[1]], axis=1)
        psend[...] = both.astype(bf16).reshape(psend.shape)
        gpart[...] = pack_gram(gram).reshape(gpart.shape)
        each_owner(owners, lambda o: p1(o, me).start())
        g1.start()

    def finish_u(par):
        g1.wait_recv()
        gall[par, chip] = gpart[core] + gin[...]
        for c in chips:
            g2(par, chip, c).start()

        @pl.when(owns)
        def _():
            for d in others:
                p1(seat, d).wait_recv()
            total = psend[seat].astype(f32)
            for d in others:
                total = total + precv[d].astype(f32)
            tb[seat] = (total - ridge_value * ub[seat].astype(f32)).astype(bf16)
            far_first(lambda d: t1(seat, d).start())

        for c in chips:
            g2(par, c, chip).wait_recv()
        total = gall[par, 0]
        for c in range(1, n // 2):
            total = total + gall[par, c]
        gtot[core] = total
        g3.start()
        g3_in.wait_recv()
        ihi, ilo = split(spd_inverse(unpack_gram(gtot[...].reshape(k // 2, 2 * k))))
        none = jnp.zeros_like(ihi)
        rhs = jnp.concatenate(
            [jnp.concatenate(r, axis=1) for r in ((ihi, none), (none, ihi), (ilo, none), (none, ilo))],
            axis=0,
        )
        lhs = jnp.concatenate(
            [jnp.concatenate(r, axis=1) for r in ((ihi, none, ilo, none), (none, ihi, none, ilo))], axis=0
        )
        each_owner(owners, lambda o: t1(o, me).wait_recv())
        t = tb[...].reshape(half, 2 * k)
        twice = jnp.concatenate([t, t], axis=1)
        step = mm(twice, rhs)
        step_t = mm_nt(lhs, twice)
        step_t = jnp.concatenate([step_t[:k], step_t[k:]], axis=1)
        ut[...] = (ut[...].astype(f32) + step_t).astype(bf16)
        new = (ub[...].reshape(half, 2 * k).astype(f32) + step).astype(bf16)
        ub[...] = new.reshape(ub.shape)
        u[:half] = new[:, :k]
        u[half:] = new[:, k:]

    def sent_u(par):
        g1.wait_send()
        for c in chips:
            g2(par, chip, c).wait_send()
        g3.wait_send()
        each_owner(owners, lambda o: p1(o, me).wait_send())

        @pl.when(owns)
        def _():
            for d in others:
                t1(seat, d).wait_send()

    def launch_v(par):
        now = u[...]
        now_t = ut[...]
        gu[par, my] = pack_gram(mm_nt(now_t, now_t))
        for d in rothers:
            rcopy(gu.at[par, my], gu.at[par, my], gus.at[d], gur.at[par, my], "run", d).start()
        for c in range(vchunks):
            c0, c1 = bounds[c], bounds[c + 1]
            fit = mm(now, vt[:, c0:c1])
            pv[c][par, my] = mm(now_t, resid(c0, c1, fit)).astype(bf16)
            for d in rothers:
                mine = pv[c].at[par, my]
                rcopy(mine, mine, pvs.at[d, c], pvr.at[par, my, c], "run", d).start()
        sent_u(par)
        for d in rothers:
            rcopy(gu.at[par, my], gu.at[par, d], gus.at[d], gur.at[par, d], "run", d).wait()
        total = gu[par, 0]
        for d in range(1, nr):
            total = total + gu[par, d]
        ihi, ilo = split(spd_inverse(unpack_gram(total)))
        lhs = jnp.concatenate([ihi, ilo, ihi], axis=1)

        def update(c):
            c0, c1 = bounds[c], bounds[c + 1]
            for d in rothers:
                rcopy(
                    pv[c].at[par, my], pv[c].at[par, d], pvs.at[d, c], pvr.at[par, d, c], "run", d
                ).wait()
            share = pv[c][par, 0].astype(f32)
            for d in range(1, nr):
                share = share + pv[c][par, d].astype(f32)
            old = vt[:, c0:c1].astype(f32)
            dhi, dlo = split(share - ridge_value * old)
            step = mm(lhs, jnp.concatenate([dhi, dhi, dlo], axis=0))
            vt[:, c0:c1] = (old + step).astype(bf16)

        return update

    pl.semaphore_wait(barrier, n - 1 + nr - 1)
    launch_u(None, 0)

    def iteration(it, carry):
        par = lax.rem(it, 2)
        finish_u(par)
        launch_u(launch_v(par), 1 - par)
        return carry

    lax.fori_loop(0, ITERS - 1, iteration, 0)
    finish_u((ITERS - 1) % 2)
    update = launch_v((ITERS - 1) % 2)
    for c in range(vchunks):
        c0, c1 = bounds[c], bounds[c + 1]
        update(c)
        fit = mm(u[...], vt[:, c0:c1]).astype(bf16)
        x = x_ref[:, c0:c1]
        out_ref[:, c0:c1] = jnp.where(x < present, x, fit)


def chunk_bounds(cols):
    unit = cols // CHUNK_PARTS
    if unit % 128:
        return (0, cols)
    return tuple(unit * c for c in CHUNK_CUTS)


def local(n, nr, intensity, observed, run_factors, prec_factors):
    rows, cols = intensity.shape
    words = observed.shape[1]
    k = run_factors.shape[1]
    half = rows // 2
    owners = max(1, min(n // 2, half // 32))
    sp = half // owners
    bounds = chunk_bounds(cols)
    vchunks = len(bounds) - 1
    nb = max(1, rows // 128)
    dma = pltpu.SemaphoreType.DMA
    hbm = pl.BlockSpec(memory_space=pltpu.HBM)
    operands = (intensity, observed, run_factors.T, prec_factors.T)
    return pl.pallas_call(
        functools.partial(als_kernel, n, nr, owners, bounds),
        out_shape=jax.ShapeDtypeStruct((rows, cols), bf16),
        in_specs=[hbm] * 4,
        out_specs=pl.BlockSpec(memory_space=pltpu.VMEM),
        scratch_shapes=[
            pltpu.VMEM((rows, cols), bf16),
            pltpu.VMEM((rows, words), jnp.int32),
            pltpu.VMEM((k, rows), bf16),
            pltpu.VMEM((rows, k), bf16),
            pltpu.VMEM((owners, sp, 2 * k), bf16),
            pltpu.VMEM((k, cols), bf16),
            pltpu.VMEM((2, half, k), f32),
            pltpu.VMEM((2, k // 4, 2 * k), f32),
            pltpu.VMEM((k // 4, 2 * k), f32),
            pltpu.VMEM((2, n // 2, k // 4, 2 * k), f32),
            pltpu.VMEM((2, k // 4, 2 * k), f32),
            pltpu.VMEM((owners, sp, 2 * k), bf16),
            pltpu.VMEM((n, sp, 2 * k), bf16),
            pltpu.VMEM((owners, sp, 2 * k), bf16),
            pltpu.VMEM((2, nr, k // 2, 2 * k), f32),
            [pltpu.VMEM((2, nr, k, b - a), bf16) for a, b in zip(bounds, bounds[1:])],
            dma((nb,)), dma((nb,)), dma((2,)),
            dma(()), dma(()), dma((n // 2,)), dma((2, n // 2)), dma(()), dma(()),
            dma((owners,)), dma((n,)), dma((n,)), dma((owners,)),
            dma((nr,)), dma((2, nr)), dma((nr, vchunks)), dma((2, nr, vchunks)),
        ],
        compiler_params=pltpu.CompilerParams(
            collective_id=0, has_side_effects=True, vmem_limit_bytes=VMEM_LIMIT,
        ),
    )(*(pltpu.with_memory_space_constraint(a, pltpu.HBM) for a in operands))


def solution(mesh):
    n, nr = mesh.shape["prec"], mesh.shape["run"]
    return jax.shard_map(
        functools.partial(local, n, nr),
        mesh=mesh,
        in_specs=(P("run", "prec"), P("run", "prec"), P("run", None), P("prec", None)),
        out_specs=P("run", "prec"),
        check_vma=False,
    )
```

```python
import functools

import jax
import jax.numpy as jnp
from jax import lax
from jax.experimental import pallas as pl
from jax.experimental.pallas import tpu as pltpu
from jax.sharding import PartitionSpec as P

ITERS = 4
ridge_value = 16.0
f32 = jnp.float32
bf16 = jnp.bfloat16
MESH = pl.DeviceIdType.MESH
VMEM_LIMIT = 32 << 20
CHUNK_PARTS, CHUNK_CUTS = 4, (0, 1, 2, 3, 4)
MISSING = 2.0**100
PRESENT = 2.0**90
SCALE = 2.0**-60


def mm(a, b):
    return lax.dot_general(a, b, (((1,), (0,)), ((), ())), preferred_element_type=f32)


def mm_nt(a, b):
    return lax.dot_general(a, b, (((1,), (1,)), ((), ())), preferred_element_type=f32)


def tree_sum(terms):
    while len(terms) > 1:
        terms = [sum(terms[i : i + 2]) for i in range(0, len(terms), 2)]
    return terms[0]


def spd_inverse(a):
    size = a.shape[0]
    wide = 2 * size
    eye = (
        lax.broadcasted_iota(jnp.int32, (size, size), 0)
        == lax.broadcasted_iota(jnp.int32, (size, size), 1)
    ).astype(f32)
    full = jnp.concatenate([(a + ridge_value * eye) * SCALE, eye], axis=1)
    m = [full[i : i + 8] for i in range(0, size, 8)]
    row = lax.broadcasted_iota(jnp.int32, (8, wide), 0)

    def col(block, j):
        return jnp.broadcast_to(block[:, j : j + 1], (8, wide))

    for q in range(size // 8):
        pivot = m[q]
        cols = [col(pivot, 8 * q + j) for j in range(8)]
        for j in range(0, 8, 2):
            c0, c1 = cols[j], cols[j + 1]
            p00, p10, p01, p11 = c0[j : j + 1], c0[j + 1 : j + 2], c1[j : j + 1], c1[j + 1 : j + 2]
            inv = 1.0 / (p00 * p11 - p01 * p10)
            i00, i01, i10, i11 = p11 * inv, p01 * inv, p10 * inv, p00 * inv

            def eliminate(v):
                r0, r1 = v[j : j + 1], v[j + 1 : j + 2]
                x0, x1 = i00 * r0 - i01 * r1, i11 * r1 - i10 * r0
                rest = v - (c0 * x0 + c1 * x1)
                return jnp.where(row == j, x0, jnp.where(row == j + 1, x1, rest))

            cols = cols[: j + 2] + [eliminate(v) for v in cols[j + 2 :]]
            pivot = eliminate(pivot)
        m = [
            pivot
            if i == q
            else m[i] - tree_sum([col(m[i], 8 * q + j) * pivot[j : j + 1] for j in range(8)])
            for i in range(size // 8)
        ]
    return jnp.concatenate(m, axis=0)[:, size:] * SCALE


def split(x):
    hi = x.astype(bf16)
    return hi, (x - hi.astype(f32)).astype(bf16)


def pack_gram(g):
    h = g.shape[0] // 2
    return jnp.concatenate([g[:h], g[h:]], axis=1)


def unpack_gram(x):
    h = x.shape[1] // 2
    return jnp.concatenate([x[:, :h], x[:, h:]], axis=0)


def als_kernel(
    n, nr, owners, bounds,
    x_hbm, w_hbm, ut0_hbm, vt0_hbm, out_ref,
    x_ref, w_ref, ut, u, ub, vt, pacc, gpart, gin, gall, gtot, psend, precv, tb, gu, pv,
    xs, wsem, vs, g1s, g1r, g2s, g2r, g3s, g3r, ps, pr, ts, tr, gus, gur, pvs, pvr,
):
    me = lax.axis_index("prec")
    my = lax.axis_index("run")
    k, cols = vt.shape
    rows = u.shape[0]
    half = rows // 2
    sp = half // owners
    vchunks = len(bounds) - 1
    base, stride = n // 4, n // 2 // owners
    others = [lax.rem(me + off, n) for off in range(1, n)]
    rothers = [lax.rem(my + off, nr) for off in range(1, nr)]
    offset = me - base
    seat = lax.div(offset, stride)
    owns = (offset >= 0) & (offset < owners * stride) & (offset == seat * stride)
    core, chip = lax.rem(me, 2), lax.div(me, 2)
    chips = [lax.rem(chip + off, n // 2) for off in range(1, n // 2)]

    nb = xs.shape[0]
    rb = rows // nb
    vload = pltpu.make_async_copy(vt0_hbm, vt, vs.at[0])
    uload = pltpu.make_async_copy(ut0_hbm, ut, vs.at[1])
    xload, wload = [], []
    for i in range(nb):
        span = slice(i * rb, (i + 1) * rb)
        wload.append(pltpu.make_async_copy(w_hbm.at[span], w_ref.at[span], wsem.at[i]))
        xload.append(pltpu.make_async_copy(x_hbm.at[span], x_ref.at[span], xs.at[i]))
    vload.start()
    uload.start()
    for i in range(nb):
        wload[i].start()
        xload[i].start()
    barrier = pltpu.get_barrier_semaphore()
    for d in others:
        pl.semaphore_signal(barrier, inc=1, device_id={"prec": d}, device_id_type=MESH)
    for d in rothers:
        pl.semaphore_signal(barrier, inc=1, device_id={"run": d}, device_id_type=MESH)

    def rcopy(src, dst, ss, rs, axis, d):
        return pltpu.make_async_remote_copy(
            src_ref=src, dst_ref=dst, send_sem=ss, recv_sem=rs,
            device_id={axis: d}, device_id_type=MESH,
        )

    def place(o):
        return base + o * stride

    vload.wait()
    uload.wait()
    start = jnp.transpose(ut[...].astype(f32))
    u[...] = start.astype(bf16)
    ub[...] = (
        jnp.concatenate([start[:half], start[half:]], axis=1).astype(bf16).reshape(ub.shape)
    )

    words = w_ref.shape[1]
    wb = min(128, words)
    spread = (
        lax.broadcasted_iota(jnp.int32, (wb, 8 * wb), 0)
        == lax.broadcasted_iota(jnp.int32, (wb, 8 * wb), 1) // 8
    ).astype(f32).astype(bf16)
    bit = jnp.left_shift(1, lax.broadcasted_iota(jnp.int32, (rb, 8 * wb), 1) & 7)
    for i in range(nb):
        r0, r1 = i * rb, (i + 1) * rb
        wload[i].wait()
        xload[i].wait()
        for c in range(words // wb):
            part = w_ref[r0:r1, c * wb : (c + 1) * wb].astype(f32).astype(bf16)
            seen = (mm(part, spread).astype(jnp.int32) & bit) != 0
            x = x_ref[r0:r1, c * 8 * wb : (c + 1) * 8 * wb].astype(f32)
            x_ref[r0:r1, c * 8 * wb : (c + 1) * 8 * wb] = jnp.where(seen, x, MISSING).astype(bf16)

    present = jnp.asarray(PRESENT, bf16)

    def resid(c0, c1, fit):
        x = x_ref[:, c0:c1]
        return jnp.where(x < present, (x.astype(f32) - fit).astype(bf16), jnp.zeros_like(x))

    g1 = rcopy(gpart.at[1 - core], gin, g1s, g1r, "prec", me + 1 - 2 * core)

    g3 = rcopy(gtot.at[core], gtot.at[core], g3s, g3r, "prec", me + 1 - 2 * core)
    g3_in = rcopy(gtot.at[core], gtot.at[1 - core], g3s, g3r, "prec", me + 1 - 2 * core)

    def g2(par, o, c):
        return rcopy(gall.at[par, o], gall.at[par, o], g2s.at[c], g2r.at[par, o], "prec", 2 * c + core)

    def p1(o, d):
        return rcopy(psend.at[o], precv.at[d], ps.at[o], pr.at[d], "prec", place(o))

    def t1(o, d):
        return rcopy(tb.at[o], tb.at[o], ts.at[d], tr.at[o], "prec", d)

    def each_owner(count, act):
        def at(j):
            return jnp.where(me < n // 2, count - 1 - j, j)

        spot = at(seat)
        for j in range(count - 1):
            act(at(j + (owns & (spot <= j)).astype(jnp.int32)))

        @pl.when(jnp.logical_not(owns))
        def _():
            act(at(count - 1))

    def far_first(act):
        for j in range(n - 1):
            down = n - 1 - j
            act(jnp.where(me < n // 2, down - (down <= me).astype(jnp.int32), j + (j >= me).astype(jnp.int32)))

    def launch_u(update, par):
        gram = None
        for c in range(vchunks):
            c0, c1 = bounds[c], bounds[c + 1]
            if update is not None:
                update(c)
            v = vt[:, c0:c1]
            gram = mm_nt(v, v) if gram is None else gram + mm_nt(v, v)
            res = resid(c0, c1, mm(u[...], v))
            for h in range(2):
                proj = mm_nt(res[h * half : (h + 1) * half], v)
                pacc[h] = proj if c == 0 else pacc[h] + proj
        both = jnp.concatenate([pacc[0], pacc[1]], axis=1)
        psend[...] = both.astype(bf16).reshape(psend.shape)
        each_owner(owners, lambda o: p1(o, me).start())
        gpart[...] = pack_gram(gram).reshape(gpart.shape)
        g1.start()

    def finish_u(par):
        g1.wait_recv()
        gall[par, chip] = gpart[core] + gin[...]
        for c in chips:
            g2(par, chip, c).start()

        @pl.when(owns)
        def _():
            for d in others:
                p1(seat, d).wait_recv()
            total = psend[seat].astype(f32)
            for d in others:
                total = total + precv[d].astype(f32)
            tb[seat] = (total - ridge_value * ub[seat].astype(f32)).astype(bf16)
            far_first(lambda d: t1(seat, d).start())

        for c in chips:
            g2(par, c, chip).wait_recv()
        total = gall[par, 0]
        for c in range(1, n // 2):
            total = total + gall[par, c]
        gtot[core] = total
        g3.start()
        g3_in.wait_recv()
        ihi, ilo = split(spd_inverse(unpack_gram(gtot[...].reshape(k // 2, 2 * k))))
        none = jnp.zeros_like(ihi)
        rhs = jnp.concatenate(
            [jnp.concatenate(r, axis=1) for r in ((ihi, none), (none, ihi), (ilo, none), (none, ilo))],
            axis=0,
        )
        lhs = jnp.concatenate(
            [jnp.concatenate(r, axis=1) for r in ((ihi, none, ilo, none), (none, ihi, none, ilo))], axis=0
        )
        each_owner(owners, lambda o: t1(o, me).wait_recv())
        t = tb[...].reshape(half, 2 * k)
        twice = jnp.concatenate([t, t], axis=1)
        step = mm(twice, rhs)
        step_t = mm_nt(lhs, twice)
        step_t = jnp.concatenate([step_t[:k], step_t[k:]], axis=1)
        ut[...] = (ut[...].astype(f32) + step_t).astype(bf16)
        new = (ub[...].reshape(half, 2 * k).astype(f32) + step).astype(bf16)
        ub[...] = new.reshape(ub.shape)
        u[:half] = new[:, :k]
        u[half:] = new[:, k:]

    def sent_u(par):
        g1.wait_send()
        for c in chips:
            g2(par, chip, c).wait_send()
        g3.wait_send()
        each_owner(owners, lambda o: p1(o, me).wait_send())

        @pl.when(owns)
        def _():
            for d in others:
                t1(seat, d).wait_send()

    def launch_v(par):
        now = u[...]
        now_t = ut[...]
        gu[par, my] = pack_gram(mm_nt(now_t, now_t))
        for d in rothers:
            rcopy(gu.at[par, my], gu.at[par, my], gus.at[d], gur.at[par, my], "run", d).start()
        for c in range(vchunks):
            c0, c1 = bounds[c], bounds[c + 1]
            fit = mm(now, vt[:, c0:c1])
            pv[c][par, my] = mm(now_t, resid(c0, c1, fit)).astype(bf16)
            for d in rothers:
                mine = pv[c].at[par, my]
                rcopy(mine, mine, pvs.at[d, c], pvr.at[par, my, c], "run", d).start()
        sent_u(par)
        for d in rothers:
            rcopy(gu.at[par, my], gu.at[par, d], gus.at[d], gur.at[par, d], "run", d).wait()
        total = gu[par, 0]
        for d in range(1, nr):
            total = total + gu[par, d]
        ihi, ilo = split(spd_inverse(unpack_gram(total)))
        lhs = jnp.concatenate([ihi, ilo, ihi], axis=1)

        def update(c):
            c0, c1 = bounds[c], bounds[c + 1]
            for d in rothers:
                rcopy(
                    pv[c].at[par, my], pv[c].at[par, d], pvs.at[d, c], pvr.at[par, d, c], "run", d
                ).wait()
            share = pv[c][par, 0].astype(f32)
            for d in range(1, nr):
                share = share + pv[c][par, d].astype(f32)
            old = vt[:, c0:c1].astype(f32)
            dhi, dlo = split(share - ridge_value * old)
            step = mm(lhs, jnp.concatenate([dhi, dhi, dlo], axis=0))
            vt[:, c0:c1] = (old + step).astype(bf16)

        return update

    pl.semaphore_wait(barrier, n - 1 + nr - 1)
    launch_u(None, 0)

    def iteration(it, carry):
        par = lax.rem(it, 2)
        finish_u(par)
        launch_u(launch_v(par), 1 - par)
        return carry

    lax.fori_loop(0, ITERS - 1, iteration, 0)
    finish_u((ITERS - 1) % 2)
    update = launch_v((ITERS - 1) % 2)
    for c in range(vchunks):
        c0, c1 = bounds[c], bounds[c + 1]
        update(c)
        fit = mm(u[...], vt[:, c0:c1]).astype(bf16)
        x = x_ref[:, c0:c1]
        out_ref[:, c0:c1] = jnp.where(x < present, x, fit)


def chunk_bounds(cols):
    unit = cols // CHUNK_PARTS
    if unit % 128:
        return (0, cols)
    return tuple(unit * c for c in CHUNK_CUTS)


def local(n, nr, intensity, observed, run_factors, prec_factors):
    rows, cols = intensity.shape
    words = observed.shape[1]
    k = run_factors.shape[1]
    half = rows // 2
    owners = max(1, min(n // 2, half // 32))
    sp = half // owners
    bounds = chunk_bounds(cols)
    vchunks = len(bounds) - 1
    nb = max(1, rows // 128)
    dma = pltpu.SemaphoreType.DMA
    hbm = pl.BlockSpec(memory_space=pltpu.HBM)
    operands = (intensity, observed, run_factors.T, prec_factors.T)
    return pl.pallas_call(
        functools.partial(als_kernel, n, nr, owners, bounds),
        out_shape=jax.ShapeDtypeStruct((rows, cols), bf16),
        in_specs=[hbm] * 4,
        out_specs=pl.BlockSpec(memory_space=pltpu.VMEM),
        scratch_shapes=[
            pltpu.VMEM((rows, cols), bf16),
            pltpu.VMEM((rows, words), jnp.int32),
            pltpu.VMEM((k, rows), bf16),
            pltpu.VMEM((rows, k), bf16),
            pltpu.VMEM((owners, sp, 2 * k), bf16),
            pltpu.VMEM((k, cols), bf16),
            pltpu.VMEM((2, half, k), f32),
            pltpu.VMEM((2, k // 4, 2 * k), f32),
            pltpu.VMEM((k // 4, 2 * k), f32),
            pltpu.VMEM((2, n // 2, k // 4, 2 * k), f32),
            pltpu.VMEM((2, k // 4, 2 * k), f32),
            pltpu.VMEM((owners, sp, 2 * k), bf16),
            pltpu.VMEM((n, sp, 2 * k), bf16),
            pltpu.VMEM((owners, sp, 2 * k), bf16),
            pltpu.VMEM((2, nr, k // 2, 2 * k), f32),
            [pltpu.VMEM((2, nr, k, b - a), bf16) for a, b in zip(bounds, bounds[1:])],
            dma((nb,)), dma((nb,)), dma((2,)),
            dma(()), dma(()), dma((n // 2,)), dma((2, n // 2)), dma(()), dma(()),
            dma((owners,)), dma((n,)), dma((n,)), dma((owners,)),
            dma((nr,)), dma((2, nr)), dma((nr, vchunks)), dma((2, nr, vchunks)),
        ],
        compiler_params=pltpu.CompilerParams(
            collective_id=0, has_side_effects=True, vmem_limit_bytes=VMEM_LIMIT,
        ),
    )(*(pltpu.with_memory_space_constraint(a, pltpu.HBM) for a in operands))


def solution(mesh):
    n, nr = mesh.shape["prec"], mesh.shape["run"]
    return jax.shard_map(
        functools.partial(local, n, nr),
        mesh=mesh,
        in_specs=(P("run", "prec"), P("run", "prec"), P("run", None), P("prec", None)),
        out_specs=P("run", "prec"),
        check_vma=False,
    )
```
